256 devices in a mesh: ctx: 64 (over z, x, core), dp: 4 (over y).
Axes of the slice: x: 4, y: 4, z: 8, core: 2. Of those that a mesh axis runs over, the one named last changes fastest.
Arguments:
- query_policy: bfloat16 [4, 2, 8192, 2048], P('dp', None, 'ctx'), may hold values from -6 to 6
- key_policy: bfloat16 [4, 2, 8192, 512], P('dp', None, 'ctx'), may hold values from -6 to 6
- value_policy: bfloat16 [4, 2, 8192, 512], P('dp', None, 'ctx'), may hold values from -60 to 60
- query_reference: bfloat16 [4, 2, 8192, 2048], P('dp', None, 'ctx'), may hold values from -6 to 6
- key_reference: bfloat16 [4, 2, 8192, 512], P('dp', None, 'ctx'), may hold values from -6 to 6
- value_reference: bfloat16 [4, 2, 8192, 512], P('dp', None, 'ctx'), may hold values from -60 to 60
- readout: bfloat16 [4, 2, 8192, 2048], P('dp', None, 'ctx'), may hold values from -0.0029296875 to 0.0029296875
- response_mask: int32 [4, 2, 8192], P('dp', None, 'ctx'), may hold values from 0 to 1, as said below
Outputs:
- query_gradient_rows: bfloat16 [4, 2, 8192, 2048], P('dp', None, 'ctx')
- key_gradient_rows: bfloat16 [4, 2, 8192, 512], P('dp', None, 'ctx')
- value_gradient_rows: bfloat16 [4, 2, 8192, 512], P('dp', None, 'ctx')
- pair_loss: float32 [], replicated
The draws below stay inside these ranges and needn't reach their ends.
Inputs may be any that keep to these rules, and one draw needn't show every extreme that they name: `response_mask`: in each pair the mask is 1 exactly from the prompt's end (1 to 2048, the same for both sequences) up to but excluding the sequence's own end (4096 to 8192).
All inputs are finite; a program needn't handle non-finite values.
Results may differ from the reference program's by a relative error of at most 0.018.
Values may be sent and summed in bfloat16 or wider, within the bound.
No kernel may reach another device: no remote copies, remote signals or barrier semaphores. Data moves between devices by JAX's collectives and lax.ppermute only.
A program may use at most 192 MiB of HBM per device.

```python
import math
import jax
import jax.numpy as jnp
from jax import lax

HEADS = 16
KV_HEADS = 4
D_HEAD = 128
TOK_DEV = 128
LENGTH = 8192
PAIRS = 4
N_CTX = 64


def scaled_values(key):
    standard_key, column_key, row_key = jax.random.split(key, 3)
    full_shape = (PAIRS, 2, LENGTH, KV_HEADS * D_HEAD)
    row_shape = (PAIRS, 2, LENGTH, 1)
    standard = jnp.clip(jax.random.normal(standard_key, full_shape, jnp.float32), -6.0, 6.0)
    row_scale = jnp.exp(jax.random.uniform(row_key, row_shape, jnp.float32, math.log(0.3), math.log(3.0)))
    column_scale = jnp.exp(jax.random.uniform(column_key, (KV_HEADS * D_HEAD,), jnp.float32, 0.0, math.log(10.0))) / 3.0
    return (standard * row_scale * column_scale).astype(jnp.bfloat16)


def draw_value_policy(key, part):
    return scaled_values(jax.random.fold_in(key, 11))


def draw_value_reference(key, part):
    return scaled_values(jax.random.fold_in(key, 12))


def draw_response_mask(key, part):
    prompt_key, answer_key = jax.random.split(jax.random.fold_in(key, 13))
    prompt_end = jax.random.randint(prompt_key, (PAIRS, 1, 1), 1, LENGTH // 4 + 1)
    answer_end = jax.random.randint(answer_key, (PAIRS, 2, 1), LENGTH // 2, LENGTH + 1)
    positions = jnp.arange(LENGTH, dtype=jnp.int32)[None, None, :]
    return ((positions >= prompt_end) & (positions < answer_end)).astype(jnp.int32)


def block_scale(own_key, extent, cuts, least, high):
    level, own = 1.0, jax.random.fold_in(own_key, 6)
    for position, shards_of in cuts:
        steps = jnp.exp(jax.random.uniform(jax.random.fold_in(own, position), (shards_of,), jnp.float32, least / len(cuts), high / len(cuts)))
        level = level * jnp.repeat(steps, extent[position] // shards_of).reshape([-1 if axis == position else 1 for axis in range(len(extent))])
    return level


def normal_values(own_key, extent, deviation, limit, cuts=(), kind=jnp.bfloat16):
    values = jax.random.normal(own_key, extent, jnp.float32) * deviation
    if len(cuts) > 0:
        values = block_scale(own_key, extent, cuts, -0.22, 0.18) * values
    return jnp.clip(values, min=-limit, max=limit).astype(kind)


def setup_inputs(seed: int = 0) -> dict:
    key_list = jax.random.split(jax.random.key(seed), 9)
    query_policy = normal_values(key_list[0], (PAIRS, 2, LENGTH, HEADS * D_HEAD), 1.0, 6.0, ((0, 4), (2, 64)))
    key_policy = normal_values(key_list[1], (PAIRS, 2, LENGTH, KV_HEADS * D_HEAD), 1.0, 6.0, ((0, 4), (2, 64)))
    value_policy = draw_value_policy(jax.random.fold_in(key_list[8], 71), 0)
    query_reference = normal_values(key_list[3], (PAIRS, 2, LENGTH, HEADS * D_HEAD), 1.0, 6.0, ((0, 4), (2, 64)))
    key_reference = normal_values(key_list[4], (PAIRS, 2, LENGTH, KV_HEADS * D_HEAD), 1.0, 6.0, ((0, 4), (2, 64)))
    value_reference = draw_value_reference(jax.random.fold_in(key_list[8], 71), 0)
    readout = normal_values(key_list[6], (PAIRS, 2, LENGTH, HEADS * D_HEAD), (HEADS * D_HEAD * LENGTH // 4) ** -0.5, 0.0029296875, ((0, 4), (2, 64)))
    response_mask = draw_response_mask(jax.random.fold_in(key_list[8], 71), 0)
    return {"query_policy": query_policy, "key_policy": key_policy, "value_policy": value_policy, "query_reference": query_reference, "key_reference": key_reference, "value_reference": value_reference, "readout": readout, "response_mask": response_mask}


dpo_beta = 0.5
epsilon = 1e-06
highest_precision = lax.Precision.HIGHEST

def through_bf16(values):
    return lax.optimization_barrier(values.astype(jnp.bfloat16)).astype(jnp.float32)

def causal_mask():
    positions = jnp.arange(TOK_DEV)
    return positions[:, None] >= positions[None, :]

def split_query(block):
    return block.astype(jnp.float32).reshape(TOK_DEV, KV_HEADS, HEADS // KV_HEADS, D_HEAD)

def split_shared(block):
    return block.astype(jnp.float32).reshape(TOK_DEV, KV_HEADS, D_HEAD)

def block_state(pieces):
    key_head_rows = split_shared(pieces[0])
    value_head_rows = split_shared(pieces[1])
    return jnp.einsum('sgd,sge->gde', key_head_rows, value_head_rows, precision=highest_precision)

def block_scores(query_head_rows, key_head_rows):
    pair_score_rows = jnp.einsum('zonv,hov->onzh', query_head_rows, key_head_rows, precision=highest_precision)
    return through_bf16(jnp.where(causal_mask(), pair_score_rows, 0.0))

def block_forward(query_block, key_block, value_block, carried):
    query_head_rows = split_query(query_block)
    key_head_rows = split_shared(key_block)
    value_head_rows = split_shared(value_block)
    pair_score_rows = block_scores(query_head_rows, key_head_rows)
    carried_low = through_bf16(carried)
    unnormed_output = jnp.einsum('wmbo,owe->bwme', pair_score_rows, value_head_rows, precision=highest_precision)
    unnormed_output = unnormed_output + jnp.einsum('tgrd,gde->tgre', query_head_rows, carried_low, precision=highest_precision)
    inverse = lax.rsqrt(lax.optimization_barrier(jnp.mean(unnormed_output * unnormed_output, axis=-1, keepdims=True)) + epsilon)
    return (query_head_rows, unnormed_output * inverse, inverse)

def carried_states(key_seq, value_seq):
    states = lax.map(block_state, (key_seq, value_seq))
    totals = jnp.cumsum(states, axis=0)
    return jnp.concatenate([jnp.zeros_like(states[:1]), totals[:-1]], axis=0)

def sequence_score(inputs):
    query_seq, key_seq, value_seq, read_seq, mask_seq = inputs
    carried = carried_states(key_seq, value_seq)

    def one_block(pieces):
        query_block, key_block, value_block, carried_block, read_block, mask_block = pieces
        normed = block_forward(query_block, key_block, value_block, carried_block)[1]
        token_score = lax.optimization_barrier(jnp.sum(normed.reshape(TOK_DEV, HEADS * D_HEAD) * read_block.astype(jnp.float32), axis=-1))
        return jnp.sum(mask_block * token_score)
    return jnp.sum(lax.map(one_block, (query_seq, key_seq, value_seq, carried, read_seq, mask_seq)))

def sequence_grads(inputs):
    query_seq, key_seq, value_seq, read_seq, mask_seq, weight = inputs
    carried = carried_states(key_seq, value_seq)

    def stat_block(pieces):
        query_block, key_block, value_block, carried_block, read_block, mask_block = pieces
        query_head_rows, normed, inverse = block_forward(query_block, key_block, value_block, carried_block)
        upstream = (weight * mask_block)[:, None, None, None] * split_query(read_block)
        pulled_back_state = upstream - normed * lax.optimization_barrier(jnp.mean(upstream * normed, axis=-1, keepdims=True))
        pulled_back_state = through_bf16(pulled_back_state * inverse)
        block_grad = jnp.einsum('tgrd,tgre->gde', query_head_rows, pulled_back_state, precision=highest_precision)
        return (pulled_back_state.astype(jnp.bfloat16), block_grad)
    pulled_all, block_grads = lax.map(stat_block, (query_seq, key_seq, value_seq, carried, read_seq, mask_seq))
    suffix = jnp.cumsum(block_grads[::-1], axis=0)[::-1]
    later = jnp.concatenate([suffix[1:], jnp.zeros_like(suffix[:1])], axis=0)

    def grad_block(pieces):
        query_block, key_block, value_block, carried_block, later_block, pulled_block = pieces
        query_head_rows = split_query(query_block)
        key_head_rows = split_shared(key_block)
        value_head_rows = split_shared(value_block)
        pair_score_rows = block_scores(query_head_rows, key_head_rows)
        carried_low = through_bf16(carried_block)
        later_low = through_bf16(later_block)
        pulled_back_state = split_query(pulled_block)
        score_gradient = jnp.einsum('ivul,hvl->vuih', pulled_back_state, value_head_rows, precision=highest_precision)
        score_gradient = through_bf16(jnp.where(causal_mask(), score_gradient, 0.0))
        query_gradient_rows = jnp.einsum('wmbo,owe->bwme', score_gradient, key_head_rows, precision=highest_precision)
        query_gradient_rows = query_gradient_rows + jnp.einsum('tgre,gde->tgrd', pulled_back_state, carried_low, precision=highest_precision)
        key_gradient_rows = jnp.einsum('eacu,ceah->ueh', score_gradient, query_head_rows, precision=highest_precision)
        key_gradient_rows = key_gradient_rows + jnp.einsum('sge,gde->sgd', value_head_rows, later_low, precision=highest_precision)
        value_gradient_rows = jnp.einsum('qocz,cqok->zqk', pair_score_rows, pulled_back_state, precision=highest_precision)
        value_gradient_rows = value_gradient_rows + jnp.einsum('sgd,gde->sge', key_head_rows, later_low, precision=highest_precision)
        return (query_gradient_rows.reshape(TOK_DEV, HEADS * D_HEAD).astype(jnp.bfloat16), key_gradient_rows.reshape(TOK_DEV, KV_HEADS * D_HEAD).astype(jnp.bfloat16), value_gradient_rows.reshape(TOK_DEV, KV_HEADS * D_HEAD).astype(jnp.bfloat16))
    return lax.map(grad_block, (query_seq, key_seq, value_seq, carried, later, pulled_all.reshape(N_CTX, TOK_DEV, HEADS * D_HEAD)))

def reference(query_policy, key_policy, value_policy, query_reference, key_reference, value_reference, readout, response_mask):
    count = PAIRS * 2

    def blocks(array):
        return array.reshape(count, N_CTX, TOK_DEV, array.shape[-1])
    mask_blocks = response_mask.astype(jnp.float32).reshape(count, N_CTX, TOK_DEV)
    read_blocks = blocks(readout)
    policy_sums = lax.map(sequence_score, (blocks(query_policy), blocks(key_policy), blocks(value_policy), read_blocks, mask_blocks)).reshape(PAIRS, 2)
    reference_sums = lax.map(sequence_score, (blocks(query_reference), blocks(key_reference), blocks(value_reference), read_blocks, mask_blocks)).reshape(PAIRS, 2)
    delta = policy_sums[:, 0] - policy_sums[:, 1] - (reference_sums[:, 0] - reference_sums[:, 1])
    pair_loss = jnp.mean(jax.nn.softplus(-dpo_beta * delta))
    scale = math.sqrt(HEADS * D_HEAD * LENGTH)
    pull = dpo_beta * jax.nn.sigmoid(-dpo_beta * delta) * scale
    weights = jnp.stack([-pull, pull], axis=1).reshape(count)
    query_gradient_rows, key_gradient_rows, value_gradient_rows = lax.map(sequence_grads, (blocks(query_policy), blocks(key_policy), blocks(value_policy), read_blocks, mask_blocks, weights))
    return (query_gradient_rows.reshape(PAIRS, 2, LENGTH, HEADS * D_HEAD), key_gradient_rows.reshape(PAIRS, 2, LENGTH, KV_HEADS * D_HEAD), value_gradient_rows.reshape(PAIRS, 2, LENGTH, KV_HEADS * D_HEAD), pair_loss)
```

```python
import math

import jax
import jax.numpy as jnp
from jax import lax
from jax.experimental import pallas as pl
from jax.experimental.pallas import tpu as pltpu
from jax.sharding import Mesh, PartitionSpec as P

HEADS = 16
KV_HEADS = 4
GROUP = HEADS // KV_HEADS
D = 128
T = 128
DPO_BETA = 0.5
EPS = 1e-06
CHIPS = 32
F32 = jnp.float32
BF16 = jnp.bfloat16
SWAP = [(0, 1), (1, 0)]
SCALAR_ROWS = 8
VMEM_LIMIT = 20 * 1024 * 1024
SMALL_VMEM = 8 * 1024 * 1024


def far(*arrays):
    return tuple(pltpu.with_memory_space_constraint(x, pltpu.HBM) for x in arrays)


def near(*arrays):
    return tuple(pltpu.with_memory_space_constraint(x, pltpu.VMEM) for x in arrays)


def dot(a, b, ca, cb):
    return lax.dot_general(a, b, (((ca,), (cb,)), ((), ())), preferred_element_type=F32)


def states_kernel(core_ref, kp_ref, vp_ref, kr_ref, vr_ref, kp2_ref, vp2_ref, kr2_ref, vr2_ref, total_ref, first_ref):
    core = core_ref[0]
    sets = (
        ((kp_ref, vp_ref), (kp2_ref, vp2_ref)),
        ((kr_ref, vr_ref), (kr2_ref, vr2_ref)),
    )
    rows = 2 * KV_HEADS * D // CHIPS
    for model, (mine, theirs) in enumerate(sets):
        for g in range(KV_HEADS):
            span = slice(g * D, (g + 1) * D)
            own = dot(mine[0][0, core, :, span], mine[1][0, core, :, span], 0, 0)
            other = dot(theirs[0][0, core, :, span], theirs[1][0, core, :, span], 0, 0)
            first_ref[model, g] = jnp.where(core == 0, own, other)
            total = (own + other).astype(BF16)
            for j in range(D // rows):
                total_ref[(model * KV_HEADS + g) * (D // rows) + j] = total[j * rows : (j + 1) * rows]


def block_states(core, kp, vp, kr, vr, kp2, vp2, kr2, vr2):
    return pl.pallas_call(
        states_kernel,
        out_shape=(
            pltpu.VMEM((CHIPS, 2 * KV_HEADS * D // CHIPS, D), BF16),
            pltpu.HBM((2, KV_HEADS, D, D), F32),
        ),
        in_specs=[pl.BlockSpec(memory_space=pltpu.SMEM)] + [pl.BlockSpec(memory_space=pltpu.VMEM)] * 8,
        out_specs=(pl.BlockSpec(memory_space=pltpu.VMEM),) * 2,
        name="block_states",
        cost_estimate=pl.CostEstimate(flops=16 * 2 * D * D * T, bytes_accessed=2 << 20, transcendentals=0),
        compiler_params=pltpu.CompilerParams(vmem_limit_bytes=SMALL_VMEM),
    )(core, *far(kp, vp, kr, vr), *near(kp2, vp2, kr2, vr2))


def prefix_kernel(x_ref, o_ref):
    total = jnp.zeros(x_ref.shape[1:], F32)
    for chip in range(CHIPS):
        o_ref[chip] = total.astype(BF16)
        total = total + x_ref[chip].astype(F32)


def exclusive_prefix(x):
    return pl.pallas_call(
        prefix_kernel,
        out_shape=pltpu.VMEM(x.shape, BF16),
        in_specs=[pl.BlockSpec(memory_space=pltpu.VMEM)],
        out_specs=pl.BlockSpec(memory_space=pltpu.VMEM),
        name="exclusive_prefix",
        cost_estimate=pl.CostEstimate(flops=x.size, bytes_accessed=4 * x.size, transcendentals=0),
        compiler_params=pltpu.CompilerParams(vmem_limit_bytes=SMALL_VMEM),
    )(*near(x))


def suffix_kernel(x_ref, o_ref, delta_ref):
    rows = o_ref.shape[1]
    total = jnp.zeros((rows, D), F32)
    pieces = jnp.zeros((SCALAR_ROWS, D), F32)
    for chip in range(CHIPS - 1, -1, -1):
        o_ref[chip] = total.astype(BF16)
        total = total + x_ref[chip, 0:rows].astype(F32)
        pieces = pieces + x_ref[chip, rows : rows + SCALAR_ROWS].astype(F32)
    delta_ref[...] = jnp.broadcast_to(jnp.sum(pieces, axis=0, keepdims=True), (SCALAR_ROWS, D))


def exclusive_suffix(x):
    rows = x.shape[1] - SCALAR_ROWS
    return pl.pallas_call(
        suffix_kernel,
        out_shape=(
            pltpu.VMEM((CHIPS, rows, D), BF16),
            pltpu.VMEM((SCALAR_ROWS, D), F32),
        ),
        in_specs=[pl.BlockSpec(memory_space=pltpu.VMEM)],
        out_specs=(pl.BlockSpec(memory_space=pltpu.VMEM),) * 2,
        name="exclusive_suffix",
        cost_estimate=pl.CostEstimate(flops=x.size, bytes_accessed=4 * x.size, transcendentals=0),
        compiler_params=pltpu.CompilerParams(vmem_limit_bytes=SMALL_VMEM),
    )(*near(x))


def rows_of(x):
    return jnp.concatenate([x[:, r * D : (r + 1) * D] for r in range(GROUP)], axis=0)


def causal_rows():
    row = lax.broadcasted_iota(jnp.int32, (T, T), 0)
    column = lax.broadcasted_iota(jnp.int32, (T, T), 1)
    return jnp.concatenate([row >= column] * GROUP, axis=0)


def seq_spec(width):
    return pl.BlockSpec((1, 1, T, width), lambda g, c: (0, c[0], 0, g))


def flat_spec(width):
    return pl.BlockSpec((T, width), lambda g, c: (0, g))


def stack_spec(count, width):
    return pl.BlockSpec((count, T, width), lambda g, c: (0, 0, g))


SCORES = pl.BlockSpec((4, 1, GROUP * T, T), lambda g, c: (0, g, 0, 0))
PULLED = pl.BlockSpec((2, 1, GROUP * T, D), lambda g, c: (0, g, 0, 0))
ARBITRARY = pltpu.CompilerParams(dimension_semantics=("arbitrary",), vmem_limit_bytes=VMEM_LIMIT)


def scores_kernel(core_ref, qp_ref, qr_ref, kp_ref, kr_ref, qp2_ref, qr2_ref, kp2_ref, kr2_ref, s_ref):
    causal = causal_rows()
    pairs = (
        (qp_ref[0, 0], kp_ref[0, 0]),
        (qp2_ref[0, 0], kp2_ref[0, 0]),
        (qr_ref[0, 0], kr_ref[0, 0]),
        (qr2_ref[0, 0], kr2_ref[0, 0]),
    )
    for i, (query, key) in enumerate(pairs):
        s_ref[i, 0] = jnp.where(causal, dot(rows_of(query), key, 1, 1), 0.0).astype(BF16)


def block_scores(core, qp, qr, kp, kr, qp2, qr2, kp2, kr2):
    wide, narrow = GROUP * D, D
    return pl.pallas_call(
        scores_kernel,
        grid_spec=pltpu.PrefetchScalarGridSpec(
            num_scalar_prefetch=1,
            grid=(KV_HEADS,),
            in_specs=[
                seq_spec(wide),
                seq_spec(wide),
                seq_spec(narrow),
                seq_spec(narrow),
                seq_spec(wide),
                seq_spec(wide),
                seq_spec(narrow),
                seq_spec(narrow),
            ],
            out_specs=SCORES,
        ),
        out_shape=pltpu.HBM((4, KV_HEADS, GROUP * T, T), BF16),
        name="block_scores",
        cost_estimate=pl.CostEstimate(flops=64 * 2 * D * D * T, bytes_accessed=5 << 20, transcendentals=0),
        compiler_params=ARBITRARY,
    )(core, *far(qp, qr, kp, kr, qp2, qr2, kp2, kr2))


def forward_kernel(
    core_ref,
    qp_ref,
    qr_ref,
    vp_ref,
    vr_ref,
    read_ref,
    qp2_ref,
    qr2_ref,
    read2_ref,
    vp2_ref,
    vr2_ref,
    mask_ref,
    mask2_ref,
    s_ref,
    before_ref,
    first_ref,
    pulled_ref,
    total_ref,
    second_ref,
    carried_ref,
    acc_ref,
):
    core = core_ref[0]
    g = pl.program_id(0)
    ones = jnp.ones((D, D), BF16)

    def row_mean(x):
        return dot(x.astype(BF16), ones, 1, 0) * (1.0 / D)

    def carried_of(model):
        before = before_ref[model, 0].astype(F32)
        after = before + first_ref[model, 0]
        own = jnp.where(core == 0, before, after).astype(BF16)
        other = jnp.where(core == 0, after, before).astype(BF16)
        return own, other

    def forward(scores, query, value, carried):
        raw = dot(jnp.concatenate([scores, query], axis=1), jnp.concatenate([value, carried], axis=0), 1, 0)
        inverse = lax.rsqrt(row_mean(raw * raw) + EPS)
        return raw * inverse, inverse

    carried_policy = carried_of(0)
    carried_reference = carried_of(1)
    row = lax.broadcasted_iota(jnp.int32, (T, T), 0)
    column = lax.broadcasted_iota(jnp.int32, (T, T), 1)

    def masked(read, mask):
        mask = mask[0, pl.ds(core, 1), :].astype(F32)
        kept = jnp.sum(jnp.where(row == column, mask, 0.0), axis=1, keepdims=True)
        kept = jnp.broadcast_to(kept, (T, D))
        return jnp.concatenate([read[:, r * D : (r + 1) * D].astype(F32) * kept for r in range(GROUP)], axis=0)

    queries = rows_of(qp_ref[0, 0]), rows_of(qp2_ref[0, 0])
    queries_ref = rows_of(qr_ref[0, 0]), rows_of(qr2_ref[0, 0])
    values = vp_ref[0, 0], vp2_ref[0, 0]
    values_ref = vr_ref[0, 0], vr2_ref[0, 0]
    reads = masked(read_ref[0, 0], mask_ref), masked(read2_ref[0, 0], mask2_ref)
    tokens = jnp.zeros((1, D), F32)
    grads = []
    for i in range(2):
        read = reads[i]
        normed, inverse = forward(s_ref[i, 0], queries[i], values[i], carried_policy[i])
        normed_ref = forward(s_ref[2 + i, 0], queries_ref[i], values_ref[i], carried_reference[i])[0]
        reading = read * normed
        tokens = tokens + jnp.sum(reading - read * normed_ref, axis=0, keepdims=True)
        pulled = (inverse * (read - normed * row_mean(reading))).astype(BF16)
        pulled_ref[i, 0] = pulled
        carried_ref[i, 0] = carried_policy[i]
        grads.append(dot(queries[i], pulled, 0, 0))

    @pl.when(g == 0)
    def _():
        acc_ref[...] = jnp.zeros_like(acc_ref)

    acc_ref[0:1, :] = acc_ref[0:1, :] + tokens
    chunks = CHIPS // KV_HEADS
    total = (grads[0] + grads[1]).astype(BF16)
    rows = D // chunks
    for j in range(chunks):
        total_ref[g * chunks + j, 0:rows, :] = total[j * rows : (j + 1) * rows]
    second_ref[0] = jnp.where(core == 0, grads[1], grads[0])

    @pl.when(g == KV_HEADS - 1)
    def _():
        part = jnp.broadcast_to(jnp.sum(acc_ref[0:1, :], axis=1, keepdims=True), (SCALAR_ROWS, D))
        high = part.astype(BF16).astype(F32)
        middle = (part - high).astype(BF16).astype(F32)
        low = part - high - middle
        place = lax.broadcasted_iota(jnp.int32, (SCALAR_ROWS, D), 0)
        pieces = jnp.where(
            place == 0, high, jnp.where(place == 1, middle, jnp.where(place == 2, low, 0.0))
        ).astype(BF16)
        for chip in range(CHIPS):
            total_ref[chip, rows : rows + SCALAR_ROWS, :] = pieces


def forward_pass(core, qp, qr, vp, vr, read, qp2, qr2, read2, vp2, vr2, mask, mask2, scores, before, first):
    wide, narrow = GROUP * D, D
    state = pl.BlockSpec((2, 1, D, D), lambda g, c: (0, g, 0, 0))
    whole = pl.BlockSpec((1, 2, T), lambda g, c: (0, 0, 0))
    rows = KV_HEADS * D // CHIPS + SCALAR_ROWS
    return pl.pallas_call(
        forward_kernel,
        grid_spec=pltpu.PrefetchScalarGridSpec(
            num_scalar_prefetch=1,
            grid=(KV_HEADS,),
            in_specs=[
                seq_spec(wide),
                seq_spec(wide),
                seq_spec(narrow),
                seq_spec(narrow),
                seq_spec(wide),
                seq_spec(wide),
                seq_spec(wide),
                seq_spec(wide),
                seq_spec(narrow),
                seq_spec(narrow),
                whole,
                whole,
                SCORES,
                state,
                state,
            ],
            out_specs=(
                PULLED,
                pl.BlockSpec((CHIPS, rows, D), lambda g, c: (0, 0, 0)),
                pl.BlockSpec((1, D, D), lambda g, c: (g, 0, 0)),
                state,
            ),
            scratch_shapes=[pltpu.VMEM((8, D), F32)],
        ),
        out_shape=(
            pltpu.HBM((2, KV_HEADS, GROUP * T, D), BF16),
            pltpu.VMEM((CHIPS, rows, D), BF16),
            pltpu.HBM((KV_HEADS, D, D), F32),
            pltpu.HBM((2, KV_HEADS, D, D), BF16),
        ),
        name="forward_pass",
        cost_estimate=pl.CostEstimate(flops=192 * 2 * D * D * T, bytes_accessed=8 << 20, transcendentals=65536),
        compiler_params=ARBITRARY,
    )(core, *far(qp, qr, vp, vr, read, qp2, qr2, read2, vp2, vr2, mask, mask2, scores), *near(before), *far(first))


def backward_kernel(
    core_ref,
    qp_ref,
    kp_ref,
    vp_ref,
    qp2_ref,
    kp2_ref,
    vp2_ref,
    s_ref,
    pulled_ref,
    carried_ref,
    qg_ref,
    kv_ref,
    qg2_ref,
    kvg2_ref,
):
    causal = causal_rows()
    blocks = (
        (qp_ref[0, 0], kp_ref[0, 0], vp_ref[0, 0], qg_ref, kv_ref),
        (qp2_ref[0, 0], kp2_ref[0, 0], vp2_ref[0, 0], qg2_ref, kvg2_ref),
    )
    for i, (query, key, value, q_out, kv_out) in enumerate(blocks):
        pulled = pulled_ref[i, 0]
        dscore = jnp.where(causal, dot(pulled, value, 1, 1), 0.0).astype(BF16)
        query_grad = (dot(dscore, key, 1, 0) + dot(pulled, carried_ref[i, 0], 1, 1)).astype(BF16)
        for r in range(GROUP):
            q_out[:, r * D : (r + 1) * D] = query_grad[r * T : (r + 1) * T]
        kv_out[0] = dot(dscore, rows_of(query), 0, 0)
        kv_out[1] = dot(s_ref[i, 0], pulled, 0, 0)


def backward_pass(core, qp, kp, vp, qp2, kp2, vp2, scores, pulled, carried):
    wide, narrow = GROUP * D, D
    query_shape = pltpu.HBM((T, HEADS * D), BF16)
    pair_shape = pltpu.HBM((2, T, KV_HEADS * D), F32)
    return pl.pallas_call(
        backward_kernel,
        grid_spec=pltpu.PrefetchScalarGridSpec(
            num_scalar_prefetch=1,
            grid=(KV_HEADS,),
            in_specs=[
                seq_spec(wide),
                seq_spec(narrow),
                seq_spec(narrow),
                seq_spec(wide),
                seq_spec(narrow),
                seq_spec(narrow),
                pl.BlockSpec((2, 1, GROUP * T, T), lambda g, c: (0, g, 0, 0)),
                PULLED,
                pl.BlockSpec((2, 1, D, D), lambda g, c: (0, g, 0, 0)),
            ],
            out_specs=(flat_spec(wide), stack_spec(2, narrow), flat_spec(wide), stack_spec(2, narrow)),
        ),
        out_shape=(query_shape, pair_shape, query_shape, pair_shape),
        name="backward_pass",
        cost_estimate=pl.CostEstimate(flops=160 * 2 * D * D * T, bytes_accessed=6 << 20, transcendentals=0),
        compiler_params=ARBITRARY,
    )(core, *far(qp, kp, vp, qp2, kp2, vp2, scores, pulled, carried))


def weight_of(seq, weight_ref):
    return jnp.where(seq == 0, -weight_ref[0:1, 0:1], weight_ref[0:1, 0:1])


def scale_kernel(core_ref, own_ref, other_ref, weight_ref, o_ref):
    core = core_ref[0]
    for turn, ref in ((0, own_ref), (1, other_ref)):
        seq = lax.rem(core + turn, 2)
        o_ref[0, seq] = (ref[...].astype(F32) * weight_of(seq, weight_ref)).astype(BF16)


def scaled_queries(core, own, other, weight):
    part = pl.BlockSpec((T, GROUP * D), lambda g, c: (0, g))
    return pl.pallas_call(
        scale_kernel,
        grid_spec=pltpu.PrefetchScalarGridSpec(
            num_scalar_prefetch=1,
            grid=(KV_HEADS,),
            in_specs=[part, part, pl.BlockSpec((SCALAR_ROWS, D), lambda g, c: (0, 0))],
            out_specs=pl.BlockSpec((1, 2, T, GROUP * D), lambda g, c: (0, 0, 0, g)),
        ),
        out_shape=pltpu.HBM((1, 2, T, HEADS * D), BF16),
        name="scaled_queries",
        cost_estimate=pl.CostEstimate(flops=2 * T * HEADS * D, bytes_accessed=2 << 20, transcendentals=0),
        compiler_params=ARBITRARY,
    )(core, *far(own, other), weight)


def final_kernel(
    core_ref,
    kp_ref,
    vp_ref,
    pair_ref,
    pair2_ref,
    weight_ref,
    after_ref,
    after2_ref,
    second_ref,
    second2_ref,
    ko_ref,
    vo_ref,
):
    core = core_ref[0]
    for turn, after, second, grads_ref in (
        (0, after_ref, second_ref, pair_ref),
        (1, after2_ref, second2_ref, pair2_ref),
    ):
        seq = lax.rem(core + turn, 2)
        weight = weight_of(seq, weight_ref)
        for g in range(KV_HEADS):
            span = slice(g * D, (g + 1) * D)
            later = after[g].astype(F32)
            later = jnp.where(core == 0, later + second[g], later).astype(BF16)
            key_grad = grads_ref[0, :, span] + dot(vp_ref[0, seq, :, span], later, 1, 1)
            value_grad = grads_ref[1, :, span] + dot(kp_ref[0, seq, :, span], later, 1, 0)
            ko_ref[0, seq, :, span] = (weight * key_grad).astype(BF16)
            vo_ref[0, seq, :, span] = (weight * value_grad).astype(BF16)


def final_pass(core, kp, vp, pair, pair2, weight, after, after2, second, second2):
    shape = pltpu.HBM((1, 2, T, KV_HEADS * D), BF16)
    return pl.pallas_call(
        final_kernel,
        out_shape=(shape, shape),
        in_specs=[pl.BlockSpec(memory_space=pltpu.SMEM)] + [pl.BlockSpec(memory_space=pltpu.VMEM)] * 9,
        out_specs=(pl.BlockSpec(memory_space=pltpu.VMEM),) * 2,
        name="final_pass",
        cost_estimate=pl.CostEstimate(flops=16 * 2 * D * D * T, bytes_accessed=3 << 20, transcendentals=0),
        compiler_params=pltpu.CompilerParams(vmem_limit_bytes=SMALL_VMEM),
    )(core, *near(kp, vp, pair, pair2), weight, *near(after, after2, second, second2))


def swap(x):
    return lax.ppermute(x, "core", SWAP)


def exchange(x):
    return lax.all_to_all(x, "chip", 0, 0, tiled=True)


def shards(qp, kp, vp, qr, kr, vr, read, mask):
    core_id = lax.axis_index("core")
    core = core_id.astype(jnp.int32).reshape(1)
    first_core = core_id == 0
    kv2 = tuple(swap(x) for x in (kp, vp, kr, vr))
    kv2, wide = lax.optimization_barrier((kv2, (qp, qr, read, mask)))
    kp2, vp2, kr2, vr2 = kv2
    qp2, qr2, read2, mask2 = (swap(x) for x in wide)
    total, first = block_states(core, kp, vp, kr, vr, *kv2)
    spread = exchange(total)
    scores = block_scores(core, qp, qr, kp, kr, qp2, qr2, kp2, kr2)
    before = exchange(exclusive_prefix(spread)).reshape(2, KV_HEADS, D, D)
    pulled, payload, second, carried = forward_pass(
        core, qp, qr, vp, vr, read, qp2, qr2, read2, vp2, vr2, mask, mask2, scores, before, first
    )
    arrived = exchange(payload)
    second2 = swap(second)
    grads = backward_pass(core, qp, kp, vp, qp2, kp2, vp2, scores, pulled, carried)
    arrived, grads = lax.optimization_barrier((arrived, grads))
    qg, pair, qg2, pair2 = grads
    qg2, pair2 = swap(qg2), swap(pair2)
    after, mine = exclusive_suffix(arrived)
    after = exchange(after).reshape(KV_HEADS, D, D)

    theirs = swap(mine)
    delta = jnp.where(first_core, mine - theirs, theirs - mine)
    loss = jax.nn.softplus(-DPO_BETA * delta)
    pairs = lax.axis_size("dp")
    one, two, three = (lax.ppermute(loss, "dp", [(i, i ^ k) for i in range(pairs)]) for k in (1, 2, 3))
    pair_loss = ((loss + one) + (two + three)) / pairs
    scale = math.sqrt(HEADS * D * T * lax.axis_size("chip") * 2)
    weight = DPO_BETA * jax.nn.sigmoid(-DPO_BETA * delta) * scale
    query_rows = scaled_queries(core, qg, qg2, weight)
    after, query_rows, pair_loss, pair2, second2 = lax.optimization_barrier(
        (after, query_rows, pair_loss[0, 0], pair2, second2)
    )
    key_rows, value_rows = final_pass(core, kp, vp, pair, pair2, weight, after, swap(after), second, second2)
    return query_rows, key_rows, value_rows, pair_loss


def solution(mesh):
    devices = mesh.devices
    split = Mesh(devices.reshape(devices.shape[0] // 2, 2, devices.shape[1]), ("chip", "core", "dp"))
    placed = P("dp", None, ("chip", "core"), None)
    return jax.shard_map(
        shards,
        mesh=split,
        in_specs=(placed,) * 7 + (P("dp", None, ("chip", "core")),),
        out_specs=(placed, placed, placed, P()),
        check_vma=False,
    )
```

```python
import math

import jax
import jax.numpy as jnp
from jax import lax
from jax.experimental import pallas as pl
from jax.experimental.pallas import tpu as pltpu
from jax.sharding import Mesh, PartitionSpec as P

HEADS = 16
KV_HEADS = 4
GROUP = HEADS // KV_HEADS
D = 128
T = 128
DPO_BETA = 0.5
EPS = 1e-06
CHIPS = 32
F32 = jnp.float32
BF16 = jnp.bfloat16
SWAP = [(0, 1), (1, 0)]
SCALAR_ROWS = 8
UNROLL = 2
VMEM_LIMIT = 20 * 1024 * 1024
SMALL_VMEM = 8 * 1024 * 1024


WIDE = GROUP * D
IN_HBM = pl.BlockSpec(memory_space=pltpu.HBM)


def out_vmem(count):
    return (pl.BlockSpec(memory_space=pltpu.VMEM),) * count


def far(*arrays):
    return tuple(pltpu.with_memory_space_constraint(x, pltpu.HBM) for x in arrays)


def near(*arrays):
    return tuple(pltpu.with_memory_space_constraint(x, pltpu.VMEM) for x in arrays)


def dot(a, b, ca, cb):
    return lax.dot_general(a, b, (((ca,), (cb,)), ((), ())), preferred_element_type=F32)


def staged(moves, sems):
    copies = [pltpu.make_async_copy(a, b, sems.at[i]) for i, (a, b) in enumerate(moves)]
    for copy in copies:
        copy.start()
    return copies


def own_states_kernel(*refs):
    own_hbm, mask_hbm, mine_ref, mask_ref, own, sems = refs[:4], refs[4], refs[5], refs[6], refs[7:11], refs[11]
    core = lax.axis_index("core")
    moves = [(a.at[0, core], b) for a, b in zip(own_hbm, own)] + [(mask_hbm, mask_ref)]
    for copy in staged(moves, sems):
        copy.wait()
    for model in range(2):
        for g in range(KV_HEADS):
            span = slice(g * D, (g + 1) * D)
            mine_ref[model, g] = dot(own[2 * model][:, span], own[2 * model + 1][:, span], 0, 0)


def own_states(*arrays):
    return pl.pallas_call(
        own_states_kernel,
        out_shape=(pltpu.VMEM((2, KV_HEADS, D, D), F32), pltpu.VMEM((1, 2, T), jnp.int32)),
        in_specs=[IN_HBM] * 5,
        out_specs=out_vmem(2),
        scratch_shapes=[pltpu.VMEM((T, KV_HEADS * D), BF16)] * 4 + [pltpu.SemaphoreType.DMA((5,))],
        name="own_states",
        cost_estimate=pl.CostEstimate(flops=8 * 2 * D * D * T, bytes_accessed=1 << 20, transcendentals=0),
        compiler_params=pltpu.CompilerParams(vmem_limit_bytes=SMALL_VMEM),
    )(*far(*arrays))


def chip_states_kernel(mine_ref, kp2_ref, vp2_ref, kr2_ref, vr2_ref, total_ref):
    core = lax.axis_index("core")
    rows = 2 * KV_HEADS * D // CHIPS
    for model, (k_ref, v_ref) in enumerate(((kp2_ref, vp2_ref), (kr2_ref, vr2_ref))):
        for g in range(KV_HEADS):
            span = slice(g * D, (g + 1) * D)
            total = mine_ref[model, g] + dot(k_ref[0, core, :, span], v_ref[0, core, :, span], 0, 0)
            total = total.astype(BF16)
            for j in range(D // rows):
                total_ref[(model * KV_HEADS + g) * (D // rows) + j] = total[j * rows : (j + 1) * rows]


def chip_states(*arrays):
    return pl.pallas_call(
        chip_states_kernel,
        out_shape=pltpu.VMEM((CHIPS, 2 * KV_HEADS * D // CHIPS, D), BF16),
        in_specs=[pl.BlockSpec(memory_space=pltpu.VMEM)] * 5,
        out_specs=pl.BlockSpec(memory_space=pltpu.VMEM),
        name="chip_states",
        cost_estimate=pl.CostEstimate(flops=8 * 2 * D * D * T, bytes_accessed=1 << 20, transcendentals=0),
        compiler_params=pltpu.CompilerParams(vmem_limit_bytes=SMALL_VMEM),
    )(*near(*arrays))


def prefix_kernel(x_ref, o_ref):
    total = jnp.zeros(x_ref.shape[1:], F32)
    for chip in range(CHIPS):
        o_ref[chip] = total.astype(BF16)
        total = total + x_ref[chip].astype(F32)


def exclusive_prefix(x):
    return pl.pallas_call(
        prefix_kernel,
        out_shape=pltpu.VMEM(x.shape, BF16),
        in_specs=[pl.BlockSpec(memory_space=pltpu.VMEM)],
        out_specs=pl.BlockSpec(memory_space=pltpu.VMEM),
        name="exclusive_prefix",
        cost_estimate=pl.CostEstimate(flops=x.size, bytes_accessed=4 * x.size, transcendentals=0),
        compiler_params=pltpu.CompilerParams(vmem_limit_bytes=SMALL_VMEM),
    )(*near(x))


def suffix_kernel(x_ref, o_ref, score_ref):
    rows = o_ref.shape[1]
    total = jnp.zeros((rows, D), F32)
    pieces = jnp.zeros((SCALAR_ROWS, D), F32)
    for chip in range(CHIPS - 1, -1, -1):
        o_ref[chip] = total.astype(BF16)
        total = total + x_ref[chip, 0:rows].astype(F32)
        pieces = pieces + x_ref[chip, rows : rows + SCALAR_ROWS].astype(F32)
    score = jnp.broadcast_to(jnp.sum(pieces, axis=0, keepdims=True), (SCALAR_ROWS, D))
    score_ref[...] = jnp.where(lax.axis_index("core") == 0, score, -score)


def exclusive_suffix(x):
    rows = x.shape[1] - SCALAR_ROWS
    return pl.pallas_call(
        suffix_kernel,
        out_shape=(
            pltpu.HBM((CHIPS, rows, D), BF16),
            pltpu.VMEM((SCALAR_ROWS, D), F32),
        ),
        in_specs=[pl.BlockSpec(memory_space=pltpu.VMEM)],
        out_specs=(pl.BlockSpec(memory_space=pltpu.VMEM),) * 2,
        name="exclusive_suffix",
        cost_estimate=pl.CostEstimate(flops=x.size, bytes_accessed=4 * x.size, transcendentals=0),
        compiler_params=pltpu.CompilerParams(vmem_limit_bytes=SMALL_VMEM),
    )(*near(x))


def rows_of(x):
    return jnp.concatenate([x[:, r * D : (r + 1) * D] for r in range(GROUP)], axis=0)


def causal_rows():
    row = lax.broadcasted_iota(jnp.int32, (T, T), 0)
    column = lax.broadcasted_iota(jnp.int32, (T, T), 1)
    return jnp.concatenate([row >= column] * GROUP, axis=0)


def at(g, width):
    return pl.ds(pl.multiple_of(g * width, width), width)


def each_group(body):
    lax.fori_loop(0, KV_HEADS, lambda g, _: (body(g), 0)[1], 0, unroll=UNROLL)


def in_vmem(count):
    return [pl.BlockSpec(memory_space=pltpu.VMEM)] * count


PARAMS = pltpu.CompilerParams(vmem_limit_bytes=VMEM_LIMIT)


def forward_kernel(*refs):
    blocks = (refs[:8], refs[8:16])
    before_ref = refs[16]
    pulled_out, total_ref, second_out, carried_out = refs[17:21]
    pulled_ref, second_ref, carried_ref, acc_ref, out_sems = refs[21:]
    core = lax.axis_index("core")
    causal = causal_rows()
    row = lax.broadcasted_iota(jnp.int32, (T, T), 0)
    column = lax.broadcasted_iota(jnp.int32, (T, T), 1)
    kept = []
    for block in blocks:
        mask = block[7][0, pl.ds(core, 1), :].astype(F32)
        mask = jnp.sum(jnp.where(row == column, mask, 0.0), axis=1, keepdims=True)
        kept.append(jnp.broadcast_to(mask, (T, D)))

    def masked(read, mask):
        return jnp.concatenate([read[:, r * D : (r + 1) * D].astype(F32) * mask for r in range(GROUP)], axis=0)

    def row_mean(x):
        return jnp.sum(x, axis=1, keepdims=True) * (1.0 / D)

    def carried_of(model, g, states):
        before = before_ref[model, g].astype(F32)
        after = before + jnp.where(core == 0, states[0], states[1])
        own = jnp.where(core == 0, before, after).astype(BF16)
        other = jnp.where(core == 0, after, before).astype(BF16)
        return own, other

    def forward(scores, query, value, carried):
        raw = dot(jnp.concatenate([scores, query], axis=1), jnp.concatenate([value, carried], axis=0), 1, 0)
        inverse = lax.rsqrt(row_mean(raw * raw) + EPS)
        return raw * inverse, inverse

    acc_ref[...] = jnp.zeros_like(acc_ref)
    chunks = CHIPS // KV_HEADS
    rows = D // chunks

    def copies(g):
        return (
            pltpu.make_async_copy(pulled_ref.at[:, g], pulled_out.at[:, g], out_sems.at[0, g]),
            pltpu.make_async_copy(second_ref.at[g], second_out.at[g], out_sems.at[1, g]),
            pltpu.make_async_copy(carried_ref.at[:, g], carried_out.at[:, g], out_sems.at[2, g]),
        )

    def group(g):
        queries, keys, values, scores, carried = [], [], [], [], []
        for model in range(2):
            queries.append([rows_of(b[model][0, core, :, at(g, WIDE)]) for b in blocks])
            keys.append([b[3 + 2 * model][0, core, :, at(g, D)] for b in blocks])
            values.append([b[4 + 2 * model][0, core, :, at(g, D)] for b in blocks])
            states = [dot(k, v, 0, 0) for k, v in zip(keys[model], values[model])]
            carried.append(carried_of(model, g, states))
            scores.append(
                [jnp.where(causal, dot(q, k, 1, 1), 0.0).astype(BF16) for q, k in zip(queries[model], keys[model])]
            )
        tokens = jnp.zeros((1, D), F32)
        grads = []
        for i in range(2):
            query = queries[0][i]
            read = masked(blocks[i][2][0, core, :, at(g, WIDE)], kept[i])
            normed, inverse = forward(scores[0][i], query, values[0][i], carried[0][i])
            normed_ref = forward(scores[1][i], queries[1][i], values[1][i], carried[1][i])[0]
            reading = read * normed
            tokens = tokens + jnp.sum(reading - read * normed_ref, axis=0, keepdims=True)
            pulled = (inverse * (read - normed * row_mean(reading))).astype(BF16)
            pulled_ref[i, g] = pulled
            carried_ref[i, g] = carried[0][i]
            grads.append(dot(query, pulled, 0, 0))
        acc_ref[0:1, :] = acc_ref[0:1, :] + tokens
        total = (grads[0] + grads[1]).astype(BF16)
        for j in range(chunks):
            total_ref[g * chunks + j, 0:rows, :] = total[j * rows : (j + 1) * rows]
        second_ref[g] = jnp.where(core == 0, grads[1], grads[0])
        for copy in copies(g):
            copy.start()

    each_group(group)
    part = jnp.broadcast_to(jnp.sum(acc_ref[0:1, :], axis=1, keepdims=True), (SCALAR_ROWS, D))
    high = part.astype(BF16).astype(F32)
    middle = (part - high).astype(BF16).astype(F32)
    low = part - high - middle
    place = lax.broadcasted_iota(jnp.int32, (SCALAR_ROWS, D), 0)
    pieces = jnp.where(place == 0, high, jnp.where(place == 1, middle, jnp.where(place == 2, low, 0.0))).astype(BF16)
    for chip in range(CHIPS):
        total_ref[chip, rows : rows + SCALAR_ROWS, :] = pieces
    for g in range(KV_HEADS):
        for copy in copies(g):
            copy.wait()


def forward_pass(*arrays):
    rows = KV_HEADS * D // CHIPS + SCALAR_ROWS
    in_vmem = pl.BlockSpec(memory_space=pltpu.VMEM)
    return pl.pallas_call(
        forward_kernel,
        in_specs=[in_vmem] * 17,
        out_specs=(IN_HBM, in_vmem, IN_HBM, IN_HBM),
        out_shape=(
            pltpu.HBM((2, KV_HEADS, GROUP * T, D), BF16),
            pltpu.HBM((CHIPS, rows, D), BF16),
            pltpu.HBM((KV_HEADS, D, D), F32),
            pltpu.HBM((2, KV_HEADS, D, D), BF16),
        ),
        scratch_shapes=[
            pltpu.VMEM((2, KV_HEADS, GROUP * T, D), BF16),
            pltpu.VMEM((KV_HEADS, D, D), F32),
            pltpu.VMEM((2, KV_HEADS, D, D), BF16),
            pltpu.VMEM((8, D), F32),
            pltpu.SemaphoreType.DMA((3, KV_HEADS)),
        ],
        name="forward_pass",
        cost_estimate=pl.CostEstimate(flops=192 * 2 * D * D * T, bytes_accessed=8 << 20, transcendentals=65536),
        compiler_params=PARAMS,
    )(*near(*arrays))


def backward_kernel(*refs):
    (qp_hbm, kp_hbm, vp_hbm, qp2_hbm, kp2_hbm, vp2_hbm, pulled_hbm, carried_hbm) = refs[:8]
    qg_ref, kv_ref, qg2_ref, kvg2_ref = refs[8:12]
    qp_ref, kp_ref, vp_ref, qp2_ref, kp2_ref, vp2_ref, pulled_ref, carried_ref, sems = refs[12:]
    core = lax.axis_index("core")
    causal = causal_rows()
    moves = [
        (qp_hbm.at[0, core], qp_ref),
        (kp_hbm.at[0, core], kp_ref),
        (vp_hbm.at[0, core], vp_ref),
        (pulled_hbm, pulled_ref),
        (qp2_hbm.at[0, core], qp2_ref),
        (kp2_hbm.at[0, core], kp2_ref),
        (vp2_hbm.at[0, core], vp2_ref),
        (carried_hbm, carried_ref),
    ]
    for copy in staged(moves, sems):
        copy.wait()
    blocks = ((qp_ref, kp_ref, vp_ref, qg_ref, kv_ref), (qp2_ref, kp2_ref, vp2_ref, qg2_ref, kvg2_ref))

    def group(g):
        for i, (q_ref, k_ref, v_ref, q_out, kv_out) in enumerate(blocks):
            query, key, value = rows_of(q_ref[:, at(g, WIDE)]), k_ref[:, at(g, D)], v_ref[:, at(g, D)]
            pulled = pulled_ref[i, g]
            dscore = jnp.where(causal, dot(pulled, value, 1, 1), 0.0).astype(BF16)
            query_grad = (dot(dscore, key, 1, 0) + dot(pulled, carried_ref[i, g], 1, 1)).astype(BF16)
            q_out[:, at(g, WIDE)] = jnp.concatenate([query_grad[r * T : (r + 1) * T] for r in range(GROUP)], axis=1)
            kv_out[0, :, at(g, D)] = dot(dscore, query, 0, 0)
            scores = jnp.where(causal, dot(query, key, 1, 1), 0.0).astype(BF16)
            kv_out[1, :, at(g, D)] = dot(scores, pulled, 0, 0)

    each_group(group)


def backward_pass(*arrays):
    query_shape = pltpu.HBM((T, HEADS * D), BF16)
    pair_shape = pltpu.HBM((2, T, KV_HEADS * D), F32)
    wide, narrow = pltpu.VMEM((T, HEADS * D), BF16), pltpu.VMEM((T, KV_HEADS * D), BF16)
    return pl.pallas_call(
        backward_kernel,
        in_specs=[IN_HBM] * 8,
        out_specs=out_vmem(4),
        out_shape=(query_shape, pair_shape, query_shape, pair_shape),
        scratch_shapes=[
            wide,
            narrow,
            narrow,
            wide,
            narrow,
            narrow,
            pltpu.VMEM((2, KV_HEADS, GROUP * T, D), BF16),
            pltpu.VMEM((2, KV_HEADS, D, D), BF16),
            pltpu.SemaphoreType.DMA((8,)),
        ],
        name="backward_pass",
        cost_estimate=pl.CostEstimate(flops=160 * 2 * D * D * T, bytes_accessed=6 << 20, transcendentals=0),
        compiler_params=PARAMS,
    )(*far(*arrays))


def weight_of(seq, weight_ref):
    return jnp.where(seq == 0, -weight_ref[0:1, 0:1], weight_ref[0:1, 0:1])


def scale_kernel(own_ref, other_ref, weight_ref, o_ref):
    core = lax.axis_index("core")
    for turn, ref in ((0, own_ref), (1, other_ref)):
        seq = lax.rem(core + turn, 2)
        o_ref[0, seq] = (ref[...].astype(F32) * weight_of(seq, weight_ref)).astype(BF16)


def scaled_queries(*arrays):
    return pl.pallas_call(
        scale_kernel,
        in_specs=in_vmem(3),
        out_specs=out_vmem(1)[0],
        out_shape=pltpu.HBM((1, 2, T, HEADS * D), BF16),
        name="scaled_queries",
        cost_estimate=pl.CostEstimate(flops=2 * T * HEADS * D, bytes_accessed=2 << 20, transcendentals=0),
        compiler_params=PARAMS,
    )(*far(*arrays[:2]), arrays[2])


def final_kernel(
    kp_ref,
    vp_ref,
    pair_ref,
    pair2_ref,
    weight_ref,
    after_ref,
    after2_ref,
    second_ref,
    second2_ref,
    ko_ref,
    vo_ref,
):
    core = lax.axis_index("core")
    for turn, after, second, grads_ref in (
        (0, after_ref, second_ref, pair_ref),
        (1, after2_ref, second2_ref, pair2_ref),
    ):
        seq = lax.rem(core + turn, 2)
        weight = weight_of(seq, weight_ref)
        for g in range(KV_HEADS):
            span = slice(g * D, (g + 1) * D)
            later = after[g].astype(F32)
            later = jnp.where(core == 0, later + second[g], later).astype(BF16)
            key_grad = grads_ref[0, :, span] + dot(vp_ref[0, seq, :, span], later, 1, 1)
            value_grad = grads_ref[1, :, span] + dot(kp_ref[0, seq, :, span], later, 1, 0)
            ko_ref[0, seq, :, span] = (weight * key_grad).astype(BF16)
            vo_ref[0, seq, :, span] = (weight * value_grad).astype(BF16)


def final_pass(kp, vp, pair, pair2, weight, after, after2, second, second2):
    shape = pltpu.HBM((1, 2, T, KV_HEADS * D), BF16)
    return pl.pallas_call(
        final_kernel,
        out_shape=(shape, shape),
        in_specs=[pl.BlockSpec(memory_space=pltpu.VMEM)] * 9,
        out_specs=(pl.BlockSpec(memory_space=pltpu.VMEM),) * 2,
        name="final_pass",
        cost_estimate=pl.CostEstimate(flops=16 * 2 * D * D * T, bytes_accessed=3 << 20, transcendentals=0),
        compiler_params=pltpu.CompilerParams(vmem_limit_bytes=SMALL_VMEM),
    )(*near(kp, vp, pair, pair2), weight, *near(after, after2, second, second2))


def swap(x):
    return lax.ppermute(x, "core", SWAP)


def exchange(x):
    return lax.all_to_all(x, "chip", 0, 0, tiled=True)


def shards(qp, kp, vp, qr, kr, vr, read, mask):
    shared = tuple(swap(x) for x in (kp, vp, kr, vr, mask))
    held = own_states(kp, vp, kr, vr, mask)
    shared, (mine, mask), (qp, qr, read) = lax.optimization_barrier((shared, held, (qp, qr, read)))
    kp2, vp2, kr2, vr2, mask2 = shared
    qp2, qr2, read2 = swap(qp), swap(qr), swap(read)
    total = chip_states(mine, kp2, vp2, kr2, vr2)
    spread = exchange(total)
    before = exchange(exclusive_prefix(spread)).reshape(2, KV_HEADS, D, D)
    own = (qp, qr, read, kp, vp, kr, vr, mask)
    other = (qp2, qr2, read2, kp2, vp2, kr2, vr2, mask2)
    pulled, payload, second, carried = forward_pass(*own, *other, before)
    arrived = exchange(payload)
    second2 = swap(second)
    grads = backward_pass(qp, kp, vp, qp2, kp2, vp2, pulled, carried)
    arrived, grads = lax.optimization_barrier((arrived, grads))
    qg, pair, qg2, pair2 = grads
    qg2, pair2 = swap(qg2), swap(pair2)
    after, mine = exclusive_suffix(arrived)
    after = exchange(after).reshape(KV_HEADS, D, D)

    delta = mine + swap(mine)
    loss = jax.nn.softplus(-DPO_BETA * delta)
    pairs = lax.axis_size("dp")
    one, two, three = (lax.ppermute(loss, "dp", [(i, i ^ k) for i in range(pairs)]) for k in (1, 2, 3))
    pair_loss = ((loss + one) + (two + three)) / pairs
    scale = math.sqrt(HEADS * D * T * lax.axis_size("chip") * 2)
    weight = DPO_BETA * jax.nn.sigmoid(-DPO_BETA * delta) * scale
    query_rows = scaled_queries(qg, qg2, weight)
    after, query_rows, pair2, second2 = lax.optimization_barrier((after, query_rows, pair2, second2))
    key_rows, value_rows = final_pass(kp, vp, pair, pair2, weight, after, swap(after), second, second2)
    return query_rows, key_rows, value_rows, pair_loss[0, 0]


def solution(mesh):
    devices = mesh.devices
    split = Mesh(devices.reshape(devices.shape[0] // 2, 2, devices.shape[1]), ("chip", "core", "dp"))
    placed = P("dp", None, ("chip", "core"), None)
    return jax.shard_map(
        shards,
        mesh=split,
        in_specs=(placed,) * 7 + (P("dp", None, ("chip", "core")),),
        out_specs=(placed, placed, placed, P()),
        check_vma=False,
    )
```

```python
import math

import jax
import jax.numpy as jnp
from jax import lax
from jax.experimental import pallas as pl
from jax.experimental.pallas import tpu as pltpu
from jax.sharding import Mesh, PartitionSpec as P

HEADS = 16
KV_HEADS = 4
GROUP = HEADS // KV_HEADS
D = 128
T = 128
DPO_BETA = 0.5
EPS = 1e-06
CHIPS = 32
F32 = jnp.float32
BF16 = jnp.bfloat16
SWAP = [(0, 1), (1, 0)]
SCALAR_ROWS = 8
UNROLL = 4
VMEM_LIMIT = 20 * 1024 * 1024
SMALL_VMEM = 8 * 1024 * 1024


WIDE = GROUP * D
IN_HBM = pl.BlockSpec(memory_space=pltpu.HBM)


def out_vmem(count):
    return (pl.BlockSpec(memory_space=pltpu.VMEM),) * count


def far(*arrays):
    return tuple(pltpu.with_memory_space_constraint(x, pltpu.HBM) for x in arrays)


def near(*arrays):
    return tuple(pltpu.with_memory_space_constraint(x, pltpu.VMEM) for x in arrays)


def dot(a, b, ca, cb):
    return lax.dot_general(a, b, (((ca,), (cb,)), ((), ())), preferred_element_type=F32)


def staged(moves, sems):
    copies = [pltpu.make_async_copy(a, b, sems.at[i]) for i, (a, b) in enumerate(moves)]
    for copy in copies:
        copy.start()
    return copies


def own_states_kernel(*refs):
    own_hbm, mask_hbm, mine_ref, mask_ref, own, sems = refs[:4], refs[4], refs[5], refs[6], refs[7:11], refs[11]
    core = lax.axis_index("core")
    moves = [(a.at[0, core], b) for a, b in zip(own_hbm, own)] + [(mask_hbm, mask_ref)]
    for copy in staged(moves, sems):
        copy.wait()
    for model in range(2):
        for g in range(KV_HEADS):
            span = slice(g * D, (g + 1) * D)
            mine_ref[model, g] = dot(own[2 * model][:, span], own[2 * model + 1][:, span], 0, 0)


def own_states(*arrays):
    return pl.pallas_call(
        own_states_kernel,
        out_shape=(pltpu.VMEM((2, KV_HEADS, D, D), F32), pltpu.VMEM((1, 2, T), jnp.int32)),
        in_specs=[IN_HBM] * 5,
        out_specs=out_vmem(2),
        scratch_shapes=[pltpu.VMEM((T, KV_HEADS * D), BF16)] * 4 + [pltpu.SemaphoreType.DMA((5,))],
        name="own_states",
        cost_estimate=pl.CostEstimate(flops=8 * 2 * D * D * T, bytes_accessed=1 << 20, transcendentals=0),
        compiler_params=pltpu.CompilerParams(vmem_limit_bytes=SMALL_VMEM),
    )(*far(*arrays))


def chip_states_kernel(mine_ref, kp2_ref, vp2_ref, kr2_ref, vr2_ref, total_ref):
    core = lax.axis_index("core")
    rows = 2 * KV_HEADS * D // CHIPS
    for model, (k_ref, v_ref) in enumerate(((kp2_ref, vp2_ref), (kr2_ref, vr2_ref))):
        for g in range(KV_HEADS):
            span = slice(g * D, (g + 1) * D)
            total = mine_ref[model, g] + dot(k_ref[0, core, :, span], v_ref[0, core, :, span], 0, 0)
            total = total.astype(BF16)
            for j in range(D // rows):
                total_ref[(model * KV_HEADS + g) * (D // rows) + j] = total[j * rows : (j + 1) * rows]


def chip_states(*arrays):
    return pl.pallas_call(
        chip_states_kernel,
        out_shape=pltpu.VMEM((CHIPS, 2 * KV_HEADS * D // CHIPS, D), BF16),
        in_specs=[pl.BlockSpec(memory_space=pltpu.VMEM)] * 5,
        out_specs=pl.BlockSpec(memory_space=pltpu.VMEM),
        name="chip_states",
        cost_estimate=pl.CostEstimate(flops=8 * 2 * D * D * T, bytes_accessed=1 << 20, transcendentals=0),
        compiler_params=pltpu.CompilerParams(vmem_limit_bytes=SMALL_VMEM),
    )(*near(*arrays))


def prefix_kernel(x_ref, o_ref):
    total = jnp.zeros(x_ref.shape[1:], F32)
    for chip in range(CHIPS):
        o_ref[chip] = total.astype(BF16)
        total = total + x_ref[chip].astype(F32)


def exclusive_prefix(x):
    return pl.pallas_call(
        prefix_kernel,
        out_shape=pltpu.VMEM(x.shape, BF16),
        in_specs=[pl.BlockSpec(memory_space=pltpu.VMEM)],
        out_specs=pl.BlockSpec(memory_space=pltpu.VMEM),
        name="exclusive_prefix",
        cost_estimate=pl.CostEstimate(flops=x.size, bytes_accessed=4 * x.size, transcendentals=0),
        compiler_params=pltpu.CompilerParams(vmem_limit_bytes=SMALL_VMEM),
    )(*near(x))


def suffix_kernel(x_ref, o_ref, score_ref):
    rows = o_ref.shape[1]
    total = jnp.zeros((rows, D), F32)
    pieces = jnp.zeros((SCALAR_ROWS, D), F32)
    for chip in range(CHIPS - 1, -1, -1):
        o_ref[chip] = total.astype(BF16)
        total = total + x_ref[chip, 0:rows].astype(F32)
        pieces = pieces + x_ref[chip, rows : rows + SCALAR_ROWS].astype(F32)
    score = jnp.broadcast_to(jnp.sum(pieces, axis=0, keepdims=True), (SCALAR_ROWS, D))
    score_ref[...] = jnp.where(lax.axis_index("core") == 0, score, -score)


def exclusive_suffix(x):
    rows = x.shape[1] - SCALAR_ROWS
    return pl.pallas_call(
        suffix_kernel,
        out_shape=(
            pltpu.HBM((CHIPS, rows, D), BF16),
            pltpu.VMEM((SCALAR_ROWS, D), F32),
        ),
        in_specs=[pl.BlockSpec(memory_space=pltpu.VMEM)],
        out_specs=(pl.BlockSpec(memory_space=pltpu.VMEM),) * 2,
        name="exclusive_suffix",
        cost_estimate=pl.CostEstimate(flops=x.size, bytes_accessed=4 * x.size, transcendentals=0),
        compiler_params=pltpu.CompilerParams(vmem_limit_bytes=SMALL_VMEM),
    )(*near(x))


def rows_of(x):
    return jnp.concatenate([x[:, r * D : (r + 1) * D] for r in range(GROUP)], axis=0)


def causal_rows():
    row = lax.broadcasted_iota(jnp.int32, (T, T), 0)
    column = lax.broadcasted_iota(jnp.int32, (T, T), 1)
    return jnp.concatenate([row >= column] * GROUP, axis=0)


def at(g, width):
    return pl.ds(pl.multiple_of(g * width, width), width)


def each_group(body):
    lax.fori_loop(0, KV_HEADS, lambda g, _: (body(g), 0)[1], 0, unroll=UNROLL)


def in_vmem(count):
    return [pl.BlockSpec(memory_space=pltpu.VMEM)] * count


PARAMS = pltpu.CompilerParams(vmem_limit_bytes=VMEM_LIMIT)


def forward_kernel(*refs):
    blocks = (refs[:8], refs[8:16])
    before_ref = refs[16]
    pulled_out, total_ref, second_out, carried_out = refs[17:21]
    pulled_ref, second_ref, carried_ref, acc_ref, out_sems = refs[21:]
    core = lax.axis_index("core")
    causal = causal_rows()
    row = lax.broadcasted_iota(jnp.int32, (T, T), 0)
    column = lax.broadcasted_iota(jnp.int32, (T, T), 1)
    kept = []
    for block in blocks:
        mask = block[7][0, pl.ds(core, 1), :].astype(F32)
        mask = jnp.sum(jnp.where(row == column, mask, 0.0), axis=1, keepdims=True)
        kept.append(jnp.broadcast_to(mask, (T, D)))

    def masked(read, mask):
        return jnp.concatenate([read[:, r * D : (r + 1) * D].astype(F32) * mask for r in range(GROUP)], axis=0)

    def row_mean(x):
        return jnp.sum(x, axis=1, keepdims=True) * (1.0 / D)

    def carried_of(model, g, states):
        before = before_ref[model, g].astype(F32)
        after = before + jnp.where(core == 0, states[0], states[1])
        own = jnp.where(core == 0, before, after).astype(BF16)
        other = jnp.where(core == 0, after, before).astype(BF16)
        return own, other

    def forward(scores, query, value, carried):
        raw = dot(jnp.concatenate([scores, query], axis=1), jnp.concatenate([value, carried], axis=0), 1, 0)
        inverse = lax.rsqrt(row_mean(raw * raw) + EPS)
        return raw * inverse, inverse

    acc_ref[...] = jnp.zeros_like(acc_ref)
    chunks = CHIPS // KV_HEADS
    rows = D // chunks

    def copies(g):
        return (
            pltpu.make_async_copy(pulled_ref.at[:, g], pulled_out.at[:, g], out_sems.at[0, g]),
            pltpu.make_async_copy(second_ref.at[g], second_out.at[g], out_sems.at[1, g]),
            pltpu.make_async_copy(carried_ref.at[:, g], carried_out.at[:, g], out_sems.at[2, g]),
        )

    def group(g):
        queries, keys, values, scores, carried = [], [], [], [], []
        for model in range(2):
            queries.append([rows_of(b[model][0, core, :, at(g, WIDE)]) for b in blocks])
            keys.append([b[3 + 2 * model][0, core, :, at(g, D)] for b in blocks])
            values.append([b[4 + 2 * model][0, core, :, at(g, D)] for b in blocks])
            states = [dot(k, v, 0, 0) for k, v in zip(keys[model], values[model])]
            carried.append(carried_of(model, g, states))
            scores.append(
                [jnp.where(causal, dot(q, k, 1, 1), 0.0).astype(BF16) for q, k in zip(queries[model], keys[model])]
            )
        tokens = jnp.zeros((1, D), F32)
        grads = []
        for i in range(2):
            query = queries[0][i]
            read = masked(blocks[i][2][0, core, :, at(g, WIDE)], kept[i])
            normed, inverse = forward(scores[0][i], query, values[0][i], carried[0][i])
            normed_ref = forward(scores[1][i], queries[1][i], values[1][i], carried[1][i])[0]
            reading = read * normed
            tokens = tokens + jnp.sum(reading - read * normed_ref, axis=0, keepdims=True)
            pulled = (inverse * (read - normed * row_mean(reading))).astype(BF16)
            pulled_ref[i, g] = pulled
            carried_ref[i, g] = carried[0][i]
            grads.append(dot(query, pulled, 0, 0))
        acc_ref[0:1, :] = acc_ref[0:1, :] + tokens
        total = (grads[0] + grads[1]).astype(BF16)
        for j in range(chunks):
            total_ref[g * chunks + j, 0:rows, :] = total[j * rows : (j + 1) * rows]
        second_ref[g] = jnp.where(core == 0, grads[1], grads[0])
        for copy in copies(g):
            copy.start()

    each_group(group)
    part = jnp.broadcast_to(jnp.sum(acc_ref[0:1, :], axis=1, keepdims=True), (SCALAR_ROWS, D))
    high = part.astype(BF16).astype(F32)
    middle = (part - high).astype(BF16).astype(F32)
    low = part - high - middle
    place = lax.broadcasted_iota(jnp.int32, (SCALAR_ROWS, D), 0)
    pieces = jnp.where(place == 0, high, jnp.where(place == 1, middle, jnp.where(place == 2, low, 0.0))).astype(BF16)
    for chip in range(CHIPS):
        total_ref[chip, rows : rows + SCALAR_ROWS, :] = pieces
    for g in range(KV_HEADS):
        for copy in copies(g):
            copy.wait()


def forward_pass(*arrays):
    rows = KV_HEADS * D // CHIPS + SCALAR_ROWS
    in_vmem = pl.BlockSpec(memory_space=pltpu.VMEM)
    return pl.pallas_call(
        forward_kernel,
        in_specs=[in_vmem] * 17,
        out_specs=(IN_HBM, in_vmem, IN_HBM, IN_HBM),
        out_shape=(
            pltpu.HBM((2, KV_HEADS, GROUP * T, D), BF16),
            pltpu.HBM((CHIPS, rows, D), BF16),
            pltpu.HBM((KV_HEADS, D, D), F32),
            pltpu.HBM((2, KV_HEADS, D, D), BF16),
        ),
        scratch_shapes=[
            pltpu.VMEM((2, KV_HEADS, GROUP * T, D), BF16),
            pltpu.VMEM((KV_HEADS, D, D), F32),
            pltpu.VMEM((2, KV_HEADS, D, D), BF16),
            pltpu.VMEM((8, D), F32),
            pltpu.SemaphoreType.DMA((3, KV_HEADS)),
        ],
        name="forward_pass",
        cost_estimate=pl.CostEstimate(flops=192 * 2 * D * D * T, bytes_accessed=8 << 20, transcendentals=65536),
        compiler_params=PARAMS,
    )(*near(*arrays))


def backward_kernel(*refs):
    (qp_hbm, kp_hbm, vp_hbm, qp2_hbm, kp2_hbm, vp2_hbm, pulled_hbm, carried_hbm) = refs[:8]
    outs = refs[8:16]
    qp_ref, kp_ref, vp_ref, qp2_ref, kp2_ref, vp2_ref, pulled_ref, carried_ref = refs[16:24]
    qg_ref, pair_ref, qg2_ref, pair2_ref, in_sems, out_sems = refs[24:]
    core = lax.axis_index("core")
    causal = causal_rows()

    def load(start, count, sems):
        heads = pl.ds(start * WIDE, count * WIDE)
        shared = pl.ds(start * D, count * D)
        groups = pl.ds(start, count)
        moves = [
            (pulled_hbm.at[:, groups], pulled_ref.at[:, groups]),
            (vp_hbm.at[0, core, :, shared], vp_ref.at[:, shared]),
            (vp2_hbm.at[0, core, :, shared], vp2_ref.at[:, shared]),
            (kp_hbm.at[0, core, :, shared], kp_ref.at[:, shared]),
            (kp2_hbm.at[0, core, :, shared], kp2_ref.at[:, shared]),
            (carried_hbm.at[:, groups], carried_ref.at[:, groups]),
            (qp_hbm.at[0, core, :, heads], qp_ref.at[:, heads]),
            (qp2_hbm.at[0, core, :, heads], qp2_ref.at[:, heads]),
        ]
        return staged(moves, sems)

    def stores(g):
        heads, shared = slice(g * WIDE, (g + 1) * WIDE), slice(g * D, (g + 1) * D)
        held = (
            (qg_ref.at[:, heads], outs[0].at[:, heads]),
            (pair_ref.at[:, :, shared], outs[1].at[:, :, shared]),
            (qg2_ref.at[:, heads], outs[4 + g]),
            (pair2_ref.at[0, :, shared], outs[2].at[:, shared]),
            (pair2_ref.at[1, :, shared], outs[3].at[:, shared]),
        )
        return [pltpu.make_async_copy(a, b, out_sems.at[i, g]) for i, (a, b) in enumerate(held)]

    blocks = ((qp_ref, kp_ref, vp_ref, qg_ref, pair_ref), (qp2_ref, kp2_ref, vp2_ref, qg2_ref, pair2_ref))

    def group(g):
        heads, shared = slice(g * WIDE, (g + 1) * WIDE), slice(g * D, (g + 1) * D)
        for i, (q_ref, k_ref, v_ref, q_out, kv_out) in enumerate(blocks):
            query, key, value = rows_of(q_ref[:, heads]), k_ref[:, shared], v_ref[:, shared]
            pulled = pulled_ref[i, g]
            dscore = jnp.where(causal, dot(pulled, value, 1, 1), 0.0).astype(BF16)
            query_grad = (dot(dscore, key, 1, 0) + dot(pulled, carried_ref[i, g], 1, 1)).astype(BF16)
            q_out[:, heads] = jnp.concatenate([query_grad[r * T : (r + 1) * T] for r in range(GROUP)], axis=1)
            kv_out[0, :, shared] = dot(dscore, query, 0, 0).astype(kv_out.dtype)
            scores = jnp.where(causal, dot(query, key, 1, 1), 0.0).astype(BF16)
            kv_out[1, :, shared] = dot(scores, pulled, 0, 0).astype(kv_out.dtype)
        for copy in stores(g):
            copy.start()

    head = load(0, 1, in_sems.at[0])
    tail = load(1, KV_HEADS - 1, in_sems.at[1])
    for copy in head:
        copy.wait()
    group(0)
    for copy in tail:
        copy.wait()
    for g in range(1, KV_HEADS):
        group(g)
    for g in range(KV_HEADS):
        for copy in stores(g):
            copy.wait()


def backward_pass(*arrays):
    wide, narrow = (T, HEADS * D), (T, KV_HEADS * D)
    query, pair = pltpu.HBM(wide, BF16), pltpu.HBM((2,) + narrow, F32)
    return pl.pallas_call(
        backward_kernel,
        in_specs=[IN_HBM] * 8,
        out_specs=(IN_HBM,) * 8,
        out_shape=(query, pair) + (pltpu.HBM(narrow, BF16),) * 2 + (pltpu.HBM((T, WIDE), BF16),) * GROUP,
        scratch_shapes=[pltpu.VMEM(wide, BF16), pltpu.VMEM(narrow, BF16), pltpu.VMEM(narrow, BF16)] * 2
        + [
            pltpu.VMEM((2, KV_HEADS, GROUP * T, D), BF16),
            pltpu.VMEM((2, KV_HEADS, D, D), BF16),
        ]
        + [pltpu.VMEM(wide, BF16), pltpu.VMEM((2,) + narrow, F32), pltpu.VMEM(wide, BF16), pltpu.VMEM((2,) + narrow, BF16)]
        + [pltpu.SemaphoreType.DMA((2, 8)), pltpu.SemaphoreType.DMA((5, KV_HEADS))],
        name="backward_pass",
        cost_estimate=pl.CostEstimate(flops=192 * 2 * D * D * T, bytes_accessed=6 << 20, transcendentals=0),
        compiler_params=PARAMS,
    )(*far(*arrays))


def weight_of(seq, weight_ref):
    return jnp.where(seq == 0, -weight_ref[0:1, 0:1], weight_ref[0:1, 0:1])


def scale_kernel(own_hbm, *refs):
    others, weight_ref, o_hbm = refs[:GROUP], refs[GROUP], refs[GROUP + 1]
    own_ref, scaled_ref, in_sem, out_sems = refs[GROUP + 2 :]
    core = lax.axis_index("core")
    arriving = pltpu.make_async_copy(own_hbm, own_ref, in_sem)
    arriving.start()
    leaving = []
    for turn in (1, 0):
        if turn == 0:
            arriving.wait()
        seq = lax.rem(core + turn, 2)
        weight = weight_of(seq, weight_ref)
        for g in range(GROUP):
            heads = slice(g * WIDE, (g + 1) * WIDE)
            piece = others[g][...] if turn else own_ref[:, heads]
            scaled_ref[turn, :, heads] = (piece.astype(F32) * weight).astype(BF16)
            copy = pltpu.make_async_copy(scaled_ref.at[turn, :, heads], o_hbm.at[0, seq, :, heads], out_sems.at[turn, g])
            copy.start()
            leaving.append(copy)
    for copy in leaving:
        copy.wait()


def scaled_queries(own, others, weight):
    in_vmem = pl.BlockSpec(memory_space=pltpu.VMEM)
    return pl.pallas_call(
        scale_kernel,
        in_specs=[IN_HBM] + [in_vmem] * (GROUP + 1),
        out_specs=IN_HBM,
        out_shape=pltpu.HBM((1, 2, T, HEADS * D), BF16),
        scratch_shapes=[
            pltpu.VMEM((T, HEADS * D), BF16),
            pltpu.VMEM((2, T, HEADS * D), BF16),
            pltpu.SemaphoreType.DMA(()),
            pltpu.SemaphoreType.DMA((2, GROUP)),
        ],
        name="scaled_queries",
        cost_estimate=pl.CostEstimate(flops=2 * T * HEADS * D, bytes_accessed=T, transcendentals=0),
        compiler_params=PARAMS,
    )(*far(own), *near(*others), weight)


def shared_gradients(turn, k_ref, v_ref, grads, weight_ref, after_ref, second_ref, out_refs, hbm_refs, sems):
    core = lax.axis_index("core")
    seq = lax.rem(core + turn, 2)
    weight = weight_of(seq, weight_ref)
    for g in range(KV_HEADS):
        span = slice(g * D, (g + 1) * D)
        later = after_ref[g].astype(F32)
        later = jnp.where(core == 0, later + second_ref[g].astype(F32), later).astype(BF16)
        key_grad = grads[0][:, span].astype(F32) + dot(v_ref[0, seq, :, span], later, 1, 1)
        value_grad = grads[1][:, span].astype(F32) + dot(k_ref[0, seq, :, span], later, 1, 0)
        out_refs[0][:, span] = (weight * key_grad).astype(BF16)
        out_refs[1][:, span] = (weight * value_grad).astype(BF16)
    for copy in staged([(a, b.at[0, seq]) for a, b in zip(out_refs, hbm_refs)], sems):
        copy.wait()


def own_kernel(k_ref, v_ref, pair_ref, weight_ref, after_ref, second_ref, ko_hbm, vo_hbm, ko_ref, vo_ref, sems):
    grads = (pair_ref.at[0], pair_ref.at[1])
    shared_gradients(
        0, k_ref, v_ref, grads, weight_ref, after_ref, second_ref, (ko_ref, vo_ref), (ko_hbm, vo_hbm), sems
    )


def other_kernel(*refs):
    k_ref, v_ref, kg_ref, vg_ref, weight_ref, after_ref, second_ref, loss_ref, one_ref, two_ref, three_ref = refs[:11]
    ko_hbm, vo_hbm, pair_loss_ref, ko_ref, vo_ref, sems = refs[13:]
    pairs = lax.axis_size("dp")
    loss = ((loss_ref[...] + one_ref[...]) + (two_ref[...] + three_ref[...])) / pairs
    pair_loss_ref[0, 0] = jnp.max(loss)
    shared_gradients(
        1, k_ref, v_ref, (kg_ref, vg_ref), weight_ref, after_ref, second_ref, (ko_ref, vo_ref), (ko_hbm, vo_hbm), sems
    )


ROWS = (1, 2, T, KV_HEADS * D)
FINAL = dict(
    scratch_shapes=[pltpu.VMEM(ROWS[2:], BF16)] * 2 + [pltpu.SemaphoreType.DMA((2,))],
    cost_estimate=pl.CostEstimate(flops=8 * 2 * D * D * T, bytes_accessed=1 << 20, transcendentals=0),
    compiler_params=pltpu.CompilerParams(vmem_limit_bytes=SMALL_VMEM),
)


def own_gradients(*arrays):
    return pl.pallas_call(
        own_kernel,
        in_specs=list(out_vmem(6)),
        out_specs=(IN_HBM,) * 2,
        out_shape=(pltpu.HBM(ROWS, BF16),) * 2,
        name="own_gradients",
        **FINAL,
    )(*near(*arrays))


def other_gradients(*arrays):
    return pl.pallas_call(
        other_kernel,
        in_specs=list(out_vmem(11)) + [IN_HBM] * 2,
        out_specs=(IN_HBM, IN_HBM, pl.BlockSpec(memory_space=pltpu.SMEM)),
        out_shape=(pltpu.HBM(ROWS, BF16),) * 2 + (jax.ShapeDtypeStruct((1, 1), F32),),
        input_output_aliases={11: 0, 12: 1},
        name="other_gradients",
        **FINAL,
    )(*near(*arrays[:11]), *far(*arrays[11:]))


def swap(x):
    return lax.ppermute(x, "core", SWAP)


def exchange(x):
    return lax.all_to_all(x, "chip", 0, 0, tiled=True)


def shards(qp, kp, vp, qr, kr, vr, read, mask):
    shared = tuple(swap(x) for x in (kp, vp, kr, vr, mask))
    held = own_states(kp, vp, kr, vr, mask)
    shared, (mine, mask), (qp, qr, read) = lax.optimization_barrier((shared, held, (qp, qr, read)))
    kp2, vp2, kr2, vr2, mask2 = shared
    qp2, qr2, read2 = swap(qp), swap(qr), swap(read)
    total = chip_states(mine, kp2, vp2, kr2, vr2)
    spread = exchange(total)
    before = exchange(exclusive_prefix(spread)).reshape(2, KV_HEADS, D, D)
    own = (qp, qr, read, kp, vp, kr, vr, mask)
    other = (qp2, qr2, read2, kp2, vp2, kr2, vr2, mask2)
    pulled, payload, second, carried = forward_pass(*own, *other, before)
    arrived = exchange(payload)
    qg, pair, kg2, vg2, *qg2 = backward_pass(qp, kp, vp, qp2, kp2, vp2, pulled, carried)
    arrived, qg, pair, qg2, kg2, vg2 = lax.optimization_barrier((arrived, qg, pair, qg2, kg2, vg2))
    after, mine = exclusive_suffix(arrived)
    after, mine, qg2, kg2, vg2, second2 = lax.optimization_barrier(
        (after, mine, qg2, kg2, vg2, second.astype(BF16))
    )
    kg2, vg2, second2 = swap(kg2), swap(vg2), swap(second2)
    qg2 = tuple(swap(x) for x in qg2)
    after = exchange(after).reshape(KV_HEADS, D, D)

    delta = mine + swap(mine)
    loss = jax.nn.softplus(-DPO_BETA * delta)
    pairs = lax.axis_size("dp")
    one, two, three = (lax.ppermute(loss, "dp", [(i, i ^ k) for i in range(pairs)]) for k in (1, 2, 3))
    scale = math.sqrt(HEADS * D * T * lax.axis_size("chip") * 2)
    weight = DPO_BETA * jax.nn.sigmoid(-DPO_BETA * delta) * scale
    query_rows = scaled_queries(qg, qg2, weight)
    after, query_rows, one, two, three = lax.optimization_barrier((after, query_rows, one, two, three))
    held = own_gradients(kp, vp, pair, weight, after, second)
    key_rows, value_rows, pair_loss = other_gradients(
        kp, vp, kg2, vg2, weight, swap(after), second2, loss, one, two, three, *held
    )
    return query_rows, key_rows, value_rows, pair_loss.reshape(())


def solution(mesh):
    devices = mesh.devices
    split = Mesh(devices.reshape(devices.shape[0] // 2, 2, devices.shape[1]), ("chip", "core", "dp"))
    placed = P("dp", None, ("chip", "core"), None)
    return jax.shard_map(
        shards,
        mesh=split,
        in_specs=(placed,) * 7 + (P("dp", None, ("chip", "core")),),
        out_specs=(placed, placed, placed, P()),
        check_vma=False,
    )
```

```python
import math

import jax
import jax.numpy as jnp
from jax import lax
from jax.experimental import pallas as pl
from jax.experimental.pallas import tpu as pltpu
from jax.sharding import Mesh, PartitionSpec as P

HEADS = 16
KV_HEADS = 4
GROUP = HEADS // KV_HEADS
D = 128
T = 128
DPO_BETA = 0.5
EPS = 1e-06
CHIPS = 32
F32 = jnp.float32
BF16 = jnp.bfloat16
SWAP = [(0, 1), (1, 0)]
SCALAR_ROWS = 8
UNROLL = 4
VMEM_LIMIT = 20 * 1024 * 1024
SMALL_VMEM = 8 * 1024 * 1024


WIDE = GROUP * D
IN_HBM = pl.BlockSpec(memory_space=pltpu.HBM)


def out_vmem(count):
    return (pl.BlockSpec(memory_space=pltpu.VMEM),) * count


def far(*arrays):
    return tuple(pltpu.with_memory_space_constraint(x, pltpu.HBM) for x in arrays)


def near(*arrays):
    return tuple(pltpu.with_memory_space_constraint(x, pltpu.VMEM) for x in arrays)


def dot(a, b, ca, cb):
    return lax.dot_general(a, b, (((ca,), (cb,)), ((), ())), preferred_element_type=F32)


def staged(moves, sems):
    copies = [pltpu.make_async_copy(a, b, sems.at[i]) for i, (a, b) in enumerate(moves)]
    for copy in copies:
        copy.start()
    return copies


def own_states_kernel(*refs):
    own_hbm, mask_hbm, mine_ref, mask_ref, own, sems = refs[:4], refs[4], refs[5], refs[6], refs[7:11], refs[11]
    core = lax.axis_index("core")
    moves = [(a.at[0, core], b) for a, b in zip(own_hbm, own)] + [(mask_hbm, mask_ref)]
    for copy in staged(moves, sems):
        copy.wait()
    for model in range(2):
        for g in range(KV_HEADS):
            span = slice(g * D, (g + 1) * D)
            mine_ref[model, g] = dot(own[2 * model][:, span], own[2 * model + 1][:, span], 0, 0)


def own_states(*arrays):
    return pl.pallas_call(
        own_states_kernel,
        out_shape=(pltpu.VMEM((2, KV_HEADS, D, D), F32), pltpu.VMEM((1, 2, T), jnp.int32)),
        in_specs=[IN_HBM] * 5,
        out_specs=out_vmem(2),
        scratch_shapes=[pltpu.VMEM((T, KV_HEADS * D), BF16)] * 4 + [pltpu.SemaphoreType.DMA((5,))],
        name="own_states",
        cost_estimate=pl.CostEstimate(flops=8 * 2 * D * D * T, bytes_accessed=1 << 20, transcendentals=0),
        compiler_params=pltpu.CompilerParams(vmem_limit_bytes=SMALL_VMEM),
    )(*far(*arrays))


def chip_states_kernel(mine_ref, kp2_ref, vp2_ref, kr2_ref, vr2_ref, total_ref):
    core = lax.axis_index("core")
    rows = 2 * KV_HEADS * D // CHIPS
    for model, (k_ref, v_ref) in enumerate(((kp2_ref, vp2_ref), (kr2_ref, vr2_ref))):
        for g in range(KV_HEADS):
            span = slice(g * D, (g + 1) * D)
            total = mine_ref[model, g] + dot(k_ref[0, core, :, span], v_ref[0, core, :, span], 0, 0)
            total = total.astype(BF16)
            for j in range(D // rows):
                total_ref[(model * KV_HEADS + g) * (D // rows) + j] = total[j * rows : (j + 1) * rows]


def chip_states(*arrays):
    return pl.pallas_call(
        chip_states_kernel,
        out_shape=pltpu.VMEM((CHIPS, 2 * KV_HEADS * D // CHIPS, D), BF16),
        in_specs=[pl.BlockSpec(memory_space=pltpu.VMEM)] * 5,
        out_specs=pl.BlockSpec(memory_space=pltpu.VMEM),
        name="chip_states",
        cost_estimate=pl.CostEstimate(flops=8 * 2 * D * D * T, bytes_accessed=1 << 20, transcendentals=0),
        compiler_params=pltpu.CompilerParams(vmem_limit_bytes=SMALL_VMEM),
    )(*near(*arrays))


def prefix_kernel(x_ref, o_ref):
    total = jnp.zeros(x_ref.shape[1:], F32)
    for chip in range(CHIPS):
        o_ref[chip] = total.astype(BF16)
        total = total + x_ref[chip].astype(F32)


def exclusive_prefix(x):
    return pl.pallas_call(
        prefix_kernel,
        out_shape=pltpu.VMEM(x.shape, BF16),
        in_specs=[pl.BlockSpec(memory_space=pltpu.VMEM)],
        out_specs=pl.BlockSpec(memory_space=pltpu.VMEM),
        name="exclusive_prefix",
        cost_estimate=pl.CostEstimate(flops=x.size, bytes_accessed=4 * x.size, transcendentals=0),
        compiler_params=pltpu.CompilerParams(vmem_limit_bytes=SMALL_VMEM),
    )(*near(x))


def suffix_kernel(x_ref, o_ref, score_ref):
    rows = o_ref.shape[1]
    total = jnp.zeros((rows, D), F32)
    pieces = jnp.zeros((SCALAR_ROWS, D), F32)
    for chip in range(CHIPS - 1, -1, -1):
        o_ref[chip] = total.astype(BF16)
        total = total + x_ref[chip, 0:rows].astype(F32)
        pieces = pieces + x_ref[chip, rows : rows + SCALAR_ROWS].astype(F32)
    score = jnp.broadcast_to(jnp.sum(pieces, axis=0, keepdims=True), (SCALAR_ROWS, D))
    score_ref[...] = jnp.where(lax.axis_index("core") == 0, score, -score)


def exclusive_suffix(x):
    rows = x.shape[1] - SCALAR_ROWS
    return pl.pallas_call(
        suffix_kernel,
        out_shape=(
            pltpu.HBM((CHIPS, rows, D), BF16),
            pltpu.VMEM((SCALAR_ROWS, D), F32),
        ),
        in_specs=[pl.BlockSpec(memory_space=pltpu.VMEM)],
        out_specs=(pl.BlockSpec(memory_space=pltpu.VMEM),) * 2,
        name="exclusive_suffix",
        cost_estimate=pl.CostEstimate(flops=x.size, bytes_accessed=4 * x.size, transcendentals=0),
        compiler_params=pltpu.CompilerParams(vmem_limit_bytes=SMALL_VMEM),
    )(*near(x))


def rows_of(x):
    return jnp.concatenate([x[:, r * D : (r + 1) * D] for r in range(GROUP)], axis=0)


def causal_rows():
    row = lax.broadcasted_iota(jnp.int32, (T, T), 0)
    column = lax.broadcasted_iota(jnp.int32, (T, T), 1)
    return jnp.concatenate([row >= column] * GROUP, axis=0)


def at(g, width):
    return pl.ds(pl.multiple_of(g * width, width), width)


def each_group(body):
    lax.fori_loop(0, KV_HEADS, lambda g, _: (body(g), 0)[1], 0, unroll=UNROLL)


def in_vmem(count):
    return [pl.BlockSpec(memory_space=pltpu.VMEM)] * count


PARAMS = pltpu.CompilerParams(vmem_limit_bytes=VMEM_LIMIT)


def forward_kernel(*refs):
    blocks = (refs[:8], refs[8:16])
    before_ref = refs[16]
    pulled_out, total_ref, second_out, carried_out = refs[17:21]
    pulled_ref, second_ref, carried_ref, acc_ref, out_sems = refs[21:]
    core = lax.axis_index("core")
    causal = causal_rows()
    row = lax.broadcasted_iota(jnp.int32, (T, T), 0)
    column = lax.broadcasted_iota(jnp.int32, (T, T), 1)
    kept = []
    for block in blocks:
        mask = block[7][0, pl.ds(core, 1), :].astype(F32)
        mask = jnp.sum(jnp.where(row == column, mask, 0.0), axis=1, keepdims=True)
        kept.append(jnp.broadcast_to(mask, (T, D)))

    def masked(read, mask):
        return jnp.concatenate([read[:, r * D : (r + 1) * D].astype(F32) * mask for r in range(GROUP)], axis=0)

    def row_mean(x):
        return jnp.sum(x, axis=1, keepdims=True) * (1.0 / D)

    def carried_of(model, g, states):
        before = before_ref[model, g].astype(F32)
        after = before + jnp.where(core == 0, states[0], states[1])
        own = jnp.where(core == 0, before, after).astype(BF16)
        other = jnp.where(core == 0, after, before).astype(BF16)
        return own, other

    def forward(scores, query, value, carried):
        raw = dot(jnp.concatenate([scores, query], axis=1), jnp.concatenate([value, carried], axis=0), 1, 0)
        inverse = lax.rsqrt(row_mean(raw * raw) + EPS)
        return raw * inverse, inverse

    acc_ref[...] = jnp.zeros_like(acc_ref)
    chunks = CHIPS // KV_HEADS
    rows = D // chunks

    def copies(g):
        return (
            pltpu.make_async_copy(pulled_ref.at[:, g], pulled_out.at[:, g], out_sems.at[0, g]),
            pltpu.make_async_copy(second_ref.at[g], second_out.at[g], out_sems.at[1, g]),
            pltpu.make_async_copy(carried_ref.at[:, g], carried_out.at[:, g], out_sems.at[2, g]),
        )

    def group(g):
        queries, keys, values, scores, carried = [], [], [], [], []
        for model in range(2):
            queries.append([rows_of(b[model][0, core, :, at(g, WIDE)]) for b in blocks])
            keys.append([b[3 + 2 * model][0, core, :, at(g, D)] for b in blocks])
            values.append([b[4 + 2 * model][0, core, :, at(g, D)] for b in blocks])
            states = [dot(k, v, 0, 0) for k, v in zip(keys[model], values[model])]
            carried.append(carried_of(model, g, states))
            scores.append(
                [jnp.where(causal, dot(q, k, 1, 1), 0.0).astype(BF16) for q, k in zip(queries[model], keys[model])]
            )
        tokens = jnp.zeros((1, D), F32)
        grads = []
        for i in range(2):
            query = queries[0][i]
            read = masked(blocks[i][2][0, core, :, at(g, WIDE)], kept[i])
            normed, inverse = forward(scores[0][i], query, values[0][i], carried[0][i])
            normed_ref = forward(scores[1][i], queries[1][i], values[1][i], carried[1][i])[0]
            reading = read * normed
            tokens = tokens + jnp.sum(reading - read * normed_ref, axis=0, keepdims=True)
            pulled = (inverse * (read - normed * row_mean(reading))).astype(BF16)
            pulled_ref[i, g] = pulled
            carried_ref[i, g] = carried[0][i]
            grads.append(dot(query, pulled, 0, 0))
        acc_ref[0:1, :] = acc_ref[0:1, :] + tokens
        total = (grads[0] + grads[1]).astype(BF16)
        for j in range(chunks):
            total_ref[g * chunks + j, 0:rows, :] = total[j * rows : (j + 1) * rows]
        second_ref[g] = jnp.where(core == 0, grads[1], grads[0])
        for copy in copies(g):
            copy.start()

    each_group(group)
    part = jnp.broadcast_to(jnp.sum(acc_ref[0:1, :], axis=1, keepdims=True), (SCALAR_ROWS, D))
    high = part.astype(BF16).astype(F32)
    middle = (part - high).astype(BF16).astype(F32)
    low = part - high - middle
    place = lax.broadcasted_iota(jnp.int32, (SCALAR_ROWS, D), 0)
    pieces = jnp.where(place == 0, high, jnp.where(place == 1, middle, jnp.where(place == 2, low, 0.0))).astype(BF16)
    for chip in range(CHIPS):
        total_ref[chip, rows : rows + SCALAR_ROWS, :] = pieces
    for g in range(KV_HEADS):
        for copy in copies(g):
            copy.wait()


def forward_pass(*arrays):
    rows = KV_HEADS * D // CHIPS + SCALAR_ROWS
    in_vmem = pl.BlockSpec(memory_space=pltpu.VMEM)
    return pl.pallas_call(
        forward_kernel,
        in_specs=[in_vmem] * 17,
        out_specs=(IN_HBM, in_vmem, IN_HBM, IN_HBM),
        out_shape=(
            pltpu.HBM((2, KV_HEADS, GROUP * T, D), BF16),
            pltpu.HBM((CHIPS, rows, D), BF16),
            pltpu.HBM((KV_HEADS, D, D), F32),
            pltpu.HBM((2, KV_HEADS, D, D), BF16),
        ),
        scratch_shapes=[
            pltpu.VMEM((2, KV_HEADS, GROUP * T, D), BF16),
            pltpu.VMEM((KV_HEADS, D, D), F32),
            pltpu.VMEM((2, KV_HEADS, D, D), BF16),
            pltpu.VMEM((8, D), F32),
            pltpu.SemaphoreType.DMA((3, KV_HEADS)),
        ],
        name="forward_pass",
        cost_estimate=pl.CostEstimate(flops=192 * 2 * D * D * T, bytes_accessed=8 << 20, transcendentals=65536),
        compiler_params=PARAMS,
    )(*near(*arrays))


def backward_kernel(*refs):
    (qp_hbm, kp_hbm, vp_hbm, qp2_hbm, kp2_hbm, vp2_hbm, pulled_hbm, carried_hbm) = refs[:8]
    outs = refs[8:16]
    qp_ref, kp_ref, vp_ref, qp2_ref, kp2_ref, vp2_ref, pulled_ref, carried_ref = refs[16:24]
    qg_ref, pair_ref, qg2_ref, pair2_ref, in_sems, out_sems = refs[24:]
    core = lax.axis_index("core")
    causal = causal_rows()

    def load(start, count, sems):
        heads = pl.ds(start * WIDE, count * WIDE)
        shared = pl.ds(start * D, count * D)
        groups = pl.ds(start, count)
        moves = [
            (pulled_hbm.at[:, groups], pulled_ref.at[:, groups]),
            (vp_hbm.at[0, core, :, shared], vp_ref.at[:, shared]),
            (vp2_hbm.at[0, core, :, shared], vp2_ref.at[:, shared]),
            (kp_hbm.at[0, core, :, shared], kp_ref.at[:, shared]),
            (kp2_hbm.at[0, core, :, shared], kp2_ref.at[:, shared]),
            (carried_hbm.at[:, groups], carried_ref.at[:, groups]),
            (qp_hbm.at[0, core, :, heads], qp_ref.at[:, heads]),
            (qp2_hbm.at[0, core, :, heads], qp2_ref.at[:, heads]),
        ]
        return staged(moves, sems)

    def stores(g):
        heads, shared = slice(g * WIDE, (g + 1) * WIDE), slice(g * D, (g + 1) * D)
        held = (
            (qg_ref.at[:, heads], outs[0].at[:, heads]),
            (pair_ref.at[:, :, shared], outs[1].at[:, :, shared]),
            (qg2_ref.at[:, heads], outs[4 + g]),
            (pair2_ref.at[0, :, shared], outs[2].at[:, shared]),
            (pair2_ref.at[1, :, shared], outs[3].at[:, shared]),
        )
        return [pltpu.make_async_copy(a, b, out_sems.at[i, g]) for i, (a, b) in enumerate(held)]

    blocks = ((qp_ref, kp_ref, vp_ref, qg_ref, pair_ref), (qp2_ref, kp2_ref, vp2_ref, qg2_ref, pair2_ref))

    def group(g):
        heads, shared = slice(g * WIDE, (g + 1) * WIDE), slice(g * D, (g + 1) * D)
        for i, (q_ref, k_ref, v_ref, q_out, kv_out) in enumerate(blocks):
            query, key, value = rows_of(q_ref[:, heads]), k_ref[:, shared], v_ref[:, shared]
            pulled = pulled_ref[i, g]
            dscore = jnp.where(causal, dot(pulled, value, 1, 1), 0.0).astype(BF16)
            query_grad = (dot(dscore, key, 1, 0) + dot(pulled, carried_ref[i, g], 1, 1)).astype(BF16)
            q_out[:, heads] = jnp.concatenate([query_grad[r * T : (r + 1) * T] for r in range(GROUP)], axis=1)
            kv_out[0, :, shared] = dot(dscore, query, 0, 0).astype(kv_out.dtype)
            scores = jnp.where(causal, dot(query, key, 1, 1), 0.0).astype(BF16)
            kv_out[1, :, shared] = dot(scores, pulled, 0, 0).astype(kv_out.dtype)
        for copy in stores(g):
            copy.start()

    head = load(0, 1, in_sems.at[0])
    tail = load(1, KV_HEADS - 1, in_sems.at[1])
    for copy in head:
        copy.wait()
    group(0)
    for copy in tail:
        copy.wait()
    for g in range(1, KV_HEADS):
        group(g)
    for g in range(KV_HEADS):
        for copy in stores(g):
            copy.wait()


def backward_pass(*arrays):
    wide, narrow = (T, HEADS * D), (T, KV_HEADS * D)
    query, pair = pltpu.HBM(wide, BF16), pltpu.HBM((2,) + narrow, F32)
    return pl.pallas_call(
        backward_kernel,
        in_specs=[IN_HBM] * 8,
        out_specs=(IN_HBM,) * 8,
        out_shape=(query, pair) + (pltpu.HBM(narrow, BF16),) * 2 + (pltpu.HBM((T, WIDE), BF16),) * GROUP,
        scratch_shapes=[pltpu.VMEM(wide, BF16), pltpu.VMEM(narrow, BF16), pltpu.VMEM(narrow, BF16)] * 2
        + [
            pltpu.VMEM((2, KV_HEADS, GROUP * T, D), BF16),
            pltpu.VMEM((2, KV_HEADS, D, D), BF16),
        ]
        + [pltpu.VMEM(wide, BF16), pltpu.VMEM((2,) + narrow, F32), pltpu.VMEM(wide, BF16), pltpu.VMEM((2,) + narrow, BF16)]
        + [pltpu.SemaphoreType.DMA((2, 8)), pltpu.SemaphoreType.DMA((5, KV_HEADS))],
        name="backward_pass",
        cost_estimate=pl.CostEstimate(flops=192 * 2 * D * D * T, bytes_accessed=6 << 20, transcendentals=0),
        compiler_params=PARAMS,
    )(*far(*arrays))


def weight_of(seq, weight_ref):
    return jnp.where(seq == 0, -weight_ref[0:1, 0:1], weight_ref[0:1, 0:1])


def scale_kernel(own_hbm, *refs):
    others, weight_ref, o_hbm = refs[:GROUP], refs[GROUP], refs[GROUP + 1]
    own_ref, scaled_ref, in_sem, out_sems = refs[GROUP + 2 :]
    core = lax.axis_index("core")
    arriving = pltpu.make_async_copy(own_hbm, own_ref, in_sem)
    arriving.start()
    leaving = []
    for turn in (1, 0):
        if turn == 0:
            arriving.wait()
        seq = lax.rem(core + turn, 2)
        weight = weight_of(seq, weight_ref)
        for g in range(GROUP):
            heads = slice(g * WIDE, (g + 1) * WIDE)
            piece = others[g][...] if turn else own_ref[:, heads]
            scaled_ref[turn, :, heads] = (piece.astype(F32) * weight).astype(BF16)
            copy = pltpu.make_async_copy(scaled_ref.at[turn, :, heads], o_hbm.at[0, seq, :, heads], out_sems.at[turn, g])
            copy.start()
            leaving.append(copy)
    for copy in leaving:
        copy.wait()


def scaled_queries(own, others, weight):
    in_vmem = pl.BlockSpec(memory_space=pltpu.VMEM)
    return pl.pallas_call(
        scale_kernel,
        in_specs=[IN_HBM] + [in_vmem] * (GROUP + 1),
        out_specs=IN_HBM,
        out_shape=pltpu.HBM((1, 2, T, HEADS * D), BF16),
        scratch_shapes=[
            pltpu.VMEM((T, HEADS * D), BF16),
            pltpu.VMEM((2, T, HEADS * D), BF16),
            pltpu.SemaphoreType.DMA(()),
            pltpu.SemaphoreType.DMA((2, GROUP)),
        ],
        name="scaled_queries",
        cost_estimate=pl.CostEstimate(flops=2 * T * HEADS * D, bytes_accessed=T, transcendentals=0),
        compiler_params=PARAMS,
    )(*far(own), *near(*others), weight)


def final_kernel(*refs):
    k_ref, v_ref, pair_ref, kg2_ref, vg2_ref, weight_ref = refs[:6]
    after_ref, after2_ref, second_ref, second2_ref = refs[6:10]
    loss_ref, one_ref, two_ref, three_ref, ko_ref, vo_ref, pair_loss_ref = refs[10:]
    pairs = lax.axis_size("dp")
    loss = ((loss_ref[...] + one_ref[...]) + (two_ref[...] + three_ref[...])) / pairs
    pair_loss_ref[0, 0] = jnp.max(loss)
    core = lax.axis_index("core")
    for turn, after, second, key_part, value_part in (
        (0, after_ref, second_ref, pair_ref.at[0], pair_ref.at[1]),
        (1, after2_ref, second2_ref, kg2_ref, vg2_ref),
    ):
        seq = lax.rem(core + turn, 2)
        weight = weight_of(seq, weight_ref)
        for g in range(KV_HEADS):
            span = slice(g * D, (g + 1) * D)
            later = after[g].astype(F32)
            later = jnp.where(core == 0, later + second[g].astype(F32), later).astype(BF16)
            key_grad = key_part[:, span].astype(F32) + dot(v_ref[0, seq, :, span], later, 1, 1)
            value_grad = value_part[:, span].astype(F32) + dot(k_ref[0, seq, :, span], later, 1, 0)
            ko_ref[0, seq, :, span] = (weight * key_grad).astype(BF16)
            vo_ref[0, seq, :, span] = (weight * value_grad).astype(BF16)


def final_pass(*arrays):
    shape = pltpu.HBM((1, 2, T, KV_HEADS * D), BF16)
    return pl.pallas_call(
        final_kernel,
        in_specs=list(out_vmem(14)),
        out_specs=out_vmem(2) + (pl.BlockSpec(memory_space=pltpu.SMEM),),
        out_shape=(shape, shape, jax.ShapeDtypeStruct((1, 1), F32)),
        name="final_pass",
        cost_estimate=pl.CostEstimate(flops=16 * 2 * D * D * T, bytes_accessed=3 << 20, transcendentals=0),
        compiler_params=pltpu.CompilerParams(vmem_limit_bytes=SMALL_VMEM),
    )(*near(*arrays))


def swap(x):
    return lax.ppermute(x, "core", SWAP)


def exchange(x):
    return lax.all_to_all(x, "chip", 0, 0, tiled=True)


def shards(qp, kp, vp, qr, kr, vr, read, mask):
    shared = tuple(swap(x) for x in (kp, vp, kr, vr, mask))
    held = own_states(kp, vp, kr, vr, mask)
    shared, (mine, mask), (qp, qr, read) = lax.optimization_barrier((shared, held, (qp, qr, read)))
    kp2, vp2, kr2, vr2, mask2 = shared
    qp2, qr2, read2 = swap(qp), swap(qr), swap(read)
    total = chip_states(mine, kp2, vp2, kr2, vr2)
    spread = exchange(total)
    before = exchange(exclusive_prefix(spread)).reshape(2, KV_HEADS, D, D)
    own = (qp, qr, read, kp, vp, kr, vr, mask)
    other = (qp2, qr2, read2, kp2, vp2, kr2, vr2, mask2)
    pulled, payload, second, carried = forward_pass(*own, *other, before)
    arrived = exchange(payload)
    qg, pair, kg2, vg2, *qg2 = backward_pass(qp, kp, vp, qp2, kp2, vp2, pulled, carried)
    arrived, qg, pair, qg2, kg2, vg2 = lax.optimization_barrier((arrived, qg, pair, qg2, kg2, vg2))
    after, mine = exclusive_suffix(arrived)
    after, mine, qg2, kg2, vg2, second2 = lax.optimization_barrier(
        (after, mine, qg2, kg2, vg2, second.astype(BF16))
    )
    kg2, vg2, second2 = swap(kg2), swap(vg2), swap(second2)
    qg2 = tuple(swap(x) for x in qg2)
    after = exchange(after).reshape(KV_HEADS, D, D)

    delta = mine + swap(mine)
    loss = jax.nn.softplus(-DPO_BETA * delta)
    pairs = lax.axis_size("dp")
    one, two, three = (lax.ppermute(loss, "dp", [(i, i ^ k) for i in range(pairs)]) for k in (1, 2, 3))
    scale = math.sqrt(HEADS * D * T * lax.axis_size("chip") * 2)
    weight = DPO_BETA * jax.nn.sigmoid(-DPO_BETA * delta) * scale
    query_rows = scaled_queries(qg, qg2, weight)
    after, query_rows, one, two, three = lax.optimization_barrier((after, query_rows, one, two, three))
    key_rows, value_rows, pair_loss = final_pass(
        kp, vp, pair, kg2, vg2, weight, after, swap(after), second, second2, loss, one, two, three
    )
    return query_rows, key_rows, value_rows, pair_loss.reshape(())


def solution(mesh):
    devices = mesh.devices
    split = Mesh(devices.reshape(devices.shape[0] // 2, 2, devices.shape[1]), ("chip", "core", "dp"))
    placed = P("dp", None, ("chip", "core"), None)
    return jax.shard_map(
        shards,
        mesh=split,
        in_specs=(placed,) * 7 + (P("dp", None, ("chip", "core")),),
        out_specs=(placed, placed, placed, P()),
        check_vma=False,
    )
```

```python
import math

import jax
import jax.numpy as jnp
from jax import lax
from jax.experimental import pallas as pl
from jax.experimental.pallas import tpu as pltpu
from jax.sharding import Mesh, PartitionSpec as P

HEADS = 16
KV_HEADS = 4
GROUP = HEADS // KV_HEADS
D = 128
T = 128
DPO_BETA = 0.5
EPS = 1e-06
CHIPS = 32
F32 = jnp.float32
BF16 = jnp.bfloat16
SWAP = [(0, 1), (1, 0)]
SCALAR_ROWS = 8
UNROLL = 4
VMEM_LIMIT = 20 * 1024 * 1024
SMALL_VMEM = 8 * 1024 * 1024


WIDE = GROUP * D
IN_HBM = pl.BlockSpec(memory_space=pltpu.HBM)


def out_vmem(count):
    return (pl.BlockSpec(memory_space=pltpu.VMEM),) * count


def far(*arrays):
    return tuple(pltpu.with_memory_space_constraint(x, pltpu.HBM) for x in arrays)


def near(*arrays):
    return tuple(pltpu.with_memory_space_constraint(x, pltpu.VMEM) for x in arrays)


def dot(a, b, ca, cb):
    return lax.dot_general(a, b, (((ca,), (cb,)), ((), ())), preferred_element_type=F32)


def staged(moves, sems):
    copies = [pltpu.make_async_copy(a, b, sems.at[i]) for i, (a, b) in enumerate(moves)]
    for copy in copies:
        copy.start()
    return copies


def own_states_kernel(*refs):
    own_hbm, mask_hbm, mine_ref, mask_ref, own, sems = refs[:4], refs[4], refs[5], refs[6], refs[7:11], refs[11]
    core = lax.axis_index("core")
    moves = [(a.at[0, core], b) for a, b in zip(own_hbm, own)] + [(mask_hbm, mask_ref)]
    for copy in staged(moves, sems):
        copy.wait()
    for model in range(2):
        for g in range(KV_HEADS):
            span = slice(g * D, (g + 1) * D)
            mine_ref[model, g] = dot(own[2 * model][:, span], own[2 * model + 1][:, span], 0, 0)


def own_states(*arrays):
    return pl.pallas_call(
        own_states_kernel,
        out_shape=(pltpu.VMEM((2, KV_HEADS, D, D), F32), pltpu.VMEM((1, 2, T), jnp.int32)),
        in_specs=[IN_HBM] * 5,
        out_specs=out_vmem(2),
        scratch_shapes=[pltpu.VMEM((T, KV_HEADS * D), BF16)] * 4 + [pltpu.SemaphoreType.DMA((5,))],
        name="own_states",
        cost_estimate=pl.CostEstimate(flops=8 * 2 * D * D * T, bytes_accessed=1 << 20, transcendentals=0),
        compiler_params=pltpu.CompilerParams(vmem_limit_bytes=SMALL_VMEM),
    )(*far(*arrays))


def chip_states_kernel(mine_ref, kp2_ref, vp2_ref, kr2_ref, vr2_ref, total_ref):
    core = lax.axis_index("core")
    rows = 2 * KV_HEADS * D // CHIPS
    for model, (k_ref, v_ref) in enumerate(((kp2_ref, vp2_ref), (kr2_ref, vr2_ref))):
        for g in range(KV_HEADS):
            span = slice(g * D, (g + 1) * D)
            total = mine_ref[model, g] + dot(k_ref[0, core, :, span], v_ref[0, core, :, span], 0, 0)
            total = total.astype(BF16)
            for j in range(D // rows):
                total_ref[(model * KV_HEADS + g) * (D // rows) + j] = total[j * rows : (j + 1) * rows]


def chip_states(*arrays):
    return pl.pallas_call(
        chip_states_kernel,
        out_shape=pltpu.VMEM((CHIPS, 2 * KV_HEADS * D // CHIPS, D), BF16),
        in_specs=[pl.BlockSpec(memory_space=pltpu.VMEM)] * 5,
        out_specs=pl.BlockSpec(memory_space=pltpu.VMEM),
        name="chip_states",
        cost_estimate=pl.CostEstimate(flops=8 * 2 * D * D * T, bytes_accessed=1 << 20, transcendentals=0),
        compiler_params=pltpu.CompilerParams(vmem_limit_bytes=SMALL_VMEM),
    )(*near(*arrays))


def prefix_kernel(x_ref, o_ref):
    total = jnp.zeros(x_ref.shape[1:], F32)
    for chip in range(CHIPS):
        o_ref[chip] = total.astype(BF16)
        total = total + x_ref[chip].astype(F32)


def exclusive_prefix(x):
    return pl.pallas_call(
        prefix_kernel,
        out_shape=pltpu.VMEM(x.shape, BF16),
        in_specs=[pl.BlockSpec(memory_space=pltpu.VMEM)],
        out_specs=pl.BlockSpec(memory_space=pltpu.VMEM),
        name="exclusive_prefix",
        cost_estimate=pl.CostEstimate(flops=x.size, bytes_accessed=4 * x.size, transcendentals=0),
        compiler_params=pltpu.CompilerParams(vmem_limit_bytes=SMALL_VMEM),
    )(*near(x))


def suffix_kernel(x_ref, o_ref, score_ref):
    rows = o_ref.shape[1]
    total = jnp.zeros((rows, D), F32)
    pieces = jnp.zeros((SCALAR_ROWS, D), F32)
    for chip in range(CHIPS - 1, -1, -1):
        o_ref[chip] = total.astype(BF16)
        total = total + x_ref[chip, 0:rows].astype(F32)
        pieces = pieces + x_ref[chip, rows : rows + SCALAR_ROWS].astype(F32)
    score = jnp.broadcast_to(jnp.sum(pieces, axis=0, keepdims=True), (SCALAR_ROWS, D))
    score_ref[...] = jnp.where(lax.axis_index("core") == 0, score, -score)


def exclusive_suffix(x):
    rows = x.shape[1] - SCALAR_ROWS
    return pl.pallas_call(
        suffix_kernel,
        out_shape=(
            pltpu.HBM((CHIPS, rows, D), BF16),
            pltpu.VMEM((SCALAR_ROWS, D), F32),
        ),
        in_specs=[pl.BlockSpec(memory_space=pltpu.VMEM)],
        out_specs=(pl.BlockSpec(memory_space=pltpu.VMEM),) * 2,
        name="exclusive_suffix",
        cost_estimate=pl.CostEstimate(flops=x.size, bytes_accessed=4 * x.size, transcendentals=0),
        compiler_params=pltpu.CompilerParams(vmem_limit_bytes=SMALL_VMEM),
    )(*near(x))


def rows_of(x):
    return jnp.concatenate([x[:, r * D : (r + 1) * D] for r in range(GROUP)], axis=0)


def causal_rows():
    row = lax.broadcasted_iota(jnp.int32, (T, T), 0)
    column = lax.broadcasted_iota(jnp.int32, (T, T), 1)
    return jnp.concatenate([row >= column] * GROUP, axis=0)


def at(g, width):
    return pl.ds(pl.multiple_of(g * width, width), width)


def each_group(body):
    lax.fori_loop(0, KV_HEADS, lambda g, _: (body(g), 0)[1], 0, unroll=UNROLL)


def in_vmem(count):
    return [pl.BlockSpec(memory_space=pltpu.VMEM)] * count


PARAMS = pltpu.CompilerParams(vmem_limit_bytes=VMEM_LIMIT)


def forward_kernel(*refs):
    blocks = (refs[:8], refs[8:16])
    before_ref = refs[16]
    pulled_out, payload_out, second_out, carried_out = refs[17:21]
    pulled_ref, second_ref, carried_ref, acc_ref, total_ref, out_sems, score_sem = refs[21:]
    core = lax.axis_index("core")
    causal = causal_rows()
    row = lax.broadcasted_iota(jnp.int32, (T, T), 0)
    column = lax.broadcasted_iota(jnp.int32, (T, T), 1)
    kept = []
    for block in blocks:
        mask = block[7][0, pl.ds(core, 1), :].astype(F32)
        mask = jnp.sum(jnp.where(row == column, mask, 0.0), axis=1, keepdims=True)
        kept.append(jnp.broadcast_to(mask, (T, D)))

    def masked(read, mask):
        return jnp.concatenate([read[:, r * D : (r + 1) * D].astype(F32) * mask for r in range(GROUP)], axis=0)

    def row_mean(x):
        return jnp.sum(x, axis=1, keepdims=True) * (1.0 / D)

    def carried_of(model, g, states):
        before = before_ref[model, g].astype(F32)
        after = before + jnp.where(core == 0, states[0], states[1])
        own = jnp.where(core == 0, before, after).astype(BF16)
        other = jnp.where(core == 0, after, before).astype(BF16)
        return own, other

    def forward(scores, query, value, carried):
        raw = dot(jnp.concatenate([scores, query], axis=1), jnp.concatenate([value, carried], axis=0), 1, 0)
        inverse = lax.rsqrt(row_mean(raw * raw) + EPS)
        return raw * inverse, inverse

    acc_ref[...] = jnp.zeros_like(acc_ref)
    chunks = CHIPS // KV_HEADS
    rows = D // chunks

    def copies(g):
        return (
            pltpu.make_async_copy(
                total_ref.at[pl.ds(g * chunks, chunks), 0:rows],
                payload_out.at[pl.ds(g * chunks, chunks), 0:rows],
                out_sems.at[3, g],
            ),
            pltpu.make_async_copy(pulled_ref.at[:, g], pulled_out.at[:, g], out_sems.at[0, g]),
            pltpu.make_async_copy(second_ref.at[g], second_out.at[g], out_sems.at[1, g]),
            pltpu.make_async_copy(carried_ref.at[:, g], carried_out.at[:, g], out_sems.at[2, g]),
        )

    def group(g):
        queries, keys, values, scores, carried = [], [], [], [], []
        for model in range(2):
            queries.append([rows_of(b[model][0, core, :, at(g, WIDE)]) for b in blocks])
            keys.append([b[3 + 2 * model][0, core, :, at(g, D)] for b in blocks])
            values.append([b[4 + 2 * model][0, core, :, at(g, D)] for b in blocks])
            states = [dot(k, v, 0, 0) for k, v in zip(keys[model], values[model])]
            carried.append(carried_of(model, g, states))
            scores.append(
                [jnp.where(causal, dot(q, k, 1, 1), 0.0).astype(BF16) for q, k in zip(queries[model], keys[model])]
            )
        tokens = jnp.zeros((1, D), F32)
        grads = []
        for i in range(2):
            query = queries[0][i]
            read = masked(blocks[i][2][0, core, :, at(g, WIDE)], kept[i])
            normed, inverse = forward(scores[0][i], query, values[0][i], carried[0][i])
            normed_ref = forward(scores[1][i], queries[1][i], values[1][i], carried[1][i])[0]
            reading = read * normed
            tokens = tokens + jnp.sum(reading - read * normed_ref, axis=0, keepdims=True)
            pulled = (inverse * (read - normed * row_mean(reading))).astype(BF16)
            pulled_ref[i, g] = pulled
            carried_ref[i, g] = carried[0][i]
            grads.append(dot(query, pulled, 0, 0))
        acc_ref[0:1, :] = acc_ref[0:1, :] + tokens
        total = (grads[0] + grads[1]).astype(BF16)
        for j in range(chunks):
            total_ref[g * chunks + j, 0:rows, :] = total[j * rows : (j + 1) * rows]
        second_ref[g] = jnp.where(core == 0, grads[1], grads[0])
        for copy in copies(g):
            copy.start()

    each_group(group)
    part = jnp.broadcast_to(jnp.sum(acc_ref[0:1, :], axis=1, keepdims=True), (SCALAR_ROWS, D))
    high = part.astype(BF16).astype(F32)
    middle = (part - high).astype(BF16).astype(F32)
    low = part - high - middle
    place = lax.broadcasted_iota(jnp.int32, (SCALAR_ROWS, D), 0)
    pieces = jnp.where(place == 0, high, jnp.where(place == 1, middle, jnp.where(place == 2, low, 0.0))).astype(BF16)
    for chip in range(CHIPS):
        total_ref[chip, rows : rows + SCALAR_ROWS, :] = pieces
    scores_copy = pltpu.make_async_copy(
        total_ref.at[:, rows : rows + SCALAR_ROWS], payload_out.at[:, rows : rows + SCALAR_ROWS], score_sem
    )
    scores_copy.start()
    for g in range(KV_HEADS):
        for copy in copies(g):
            copy.wait()
    scores_copy.wait()


def forward_pass(*arrays):
    rows = KV_HEADS * D // CHIPS + SCALAR_ROWS
    in_vmem = pl.BlockSpec(memory_space=pltpu.VMEM)
    return pl.pallas_call(
        forward_kernel,
        in_specs=[in_vmem] * 17,
        out_specs=(IN_HBM,) * 4,
        out_shape=(
            pltpu.HBM((2, KV_HEADS, GROUP * T, D), BF16),
            pltpu.HBM((CHIPS, rows, D), BF16),
            pltpu.HBM((KV_HEADS, D, D), F32),
            pltpu.HBM((2, KV_HEADS, D, D), BF16),
        ),
        scratch_shapes=[
            pltpu.VMEM((2, KV_HEADS, GROUP * T, D), BF16),
            pltpu.VMEM((KV_HEADS, D, D), F32),
            pltpu.VMEM((2, KV_HEADS, D, D), BF16),
            pltpu.VMEM((8, D), F32),
            pltpu.VMEM((CHIPS, rows, D), BF16),
            pltpu.SemaphoreType.DMA((4, KV_HEADS)),
            pltpu.SemaphoreType.DMA(()),
        ],
        name="forward_pass",
        cost_estimate=pl.CostEstimate(flops=192 * 2 * D * D * T, bytes_accessed=8 << 20, transcendentals=65536),
        compiler_params=PARAMS,
    )(*near(*arrays))


def backward_kernel(*refs):
    (qp_hbm, kp_hbm, vp_hbm, qp2_hbm, kp2_hbm, vp2_hbm, pulled_hbm, carried_hbm) = refs[:8]
    outs = refs[8:16]
    qp_ref, kp_ref, vp_ref, qp2_ref, kp2_ref, vp2_ref, pulled_ref, carried_ref = refs[16:24]
    qg_ref, pair_ref, qg2_ref, pair2_ref, in_sems, out_sems = refs[24:]
    core = lax.axis_index("core")
    causal = causal_rows()

    def load(start, count, sems):
        heads = pl.ds(start * WIDE, count * WIDE)
        shared = pl.ds(start * D, count * D)
        groups = pl.ds(start, count)
        moves = [
            (pulled_hbm.at[:, groups], pulled_ref.at[:, groups]),
            (vp_hbm.at[0, core, :, shared], vp_ref.at[:, shared]),
            (vp2_hbm.at[0, core, :, shared], vp2_ref.at[:, shared]),
            (kp_hbm.at[0, core, :, shared], kp_ref.at[:, shared]),
            (kp2_hbm.at[0, core, :, shared], kp2_ref.at[:, shared]),
            (carried_hbm.at[:, groups], carried_ref.at[:, groups]),
            (qp_hbm.at[0, core, :, heads], qp_ref.at[:, heads]),
            (qp2_hbm.at[0, core, :, heads], qp2_ref.at[:, heads]),
        ]
        return staged(moves, sems)

    def stores(g):
        heads, shared = slice(g * WIDE, (g + 1) * WIDE), slice(g * D, (g + 1) * D)
        held = (
            (qg_ref.at[:, heads], outs[0].at[:, heads]),
            (pair_ref.at[:, :, shared], outs[1].at[:, :, shared]),
            (qg2_ref.at[:, heads], outs[4 + g]),
            (pair2_ref.at[0, :, shared], outs[2].at[:, shared]),
            (pair2_ref.at[1, :, shared], outs[3].at[:, shared]),
        )
        return [pltpu.make_async_copy(a, b, out_sems.at[i, g]) for i, (a, b) in enumerate(held)]

    blocks = ((qp_ref, kp_ref, vp_ref, qg_ref, pair_ref), (qp2_ref, kp2_ref, vp2_ref, qg2_ref, pair2_ref))

    def group(g):
        heads, shared = slice(g * WIDE, (g + 1) * WIDE), slice(g * D, (g + 1) * D)
        for i, (q_ref, k_ref, v_ref, q_out, kv_out) in enumerate(blocks):
            query, key, value = rows_of(q_ref[:, heads]), k_ref[:, shared], v_ref[:, shared]
            pulled = pulled_ref[i, g]
            dscore = jnp.where(causal, dot(pulled, value, 1, 1), 0.0).astype(BF16)
            query_grad = (dot(dscore, key, 1, 0) + dot(pulled, carried_ref[i, g], 1, 1)).astype(BF16)
            q_out[:, heads] = jnp.concatenate([query_grad[r * T : (r + 1) * T] for r in range(GROUP)], axis=1)
            kv_out[0, :, shared] = dot(dscore, query, 0, 0).astype(kv_out.dtype)
            scores = jnp.where(causal, dot(query, key, 1, 1), 0.0).astype(BF16)
            kv_out[1, :, shared] = dot(scores, pulled, 0, 0).astype(kv_out.dtype)
        for copy in stores(g):
            copy.start()

    head = load(0, 1, in_sems.at[0])
    tail = load(1, KV_HEADS - 1, in_sems.at[1])
    for copy in head:
        copy.wait()
    group(0)
    for copy in tail:
        copy.wait()
    for g in range(1, KV_HEADS):
        group(g)
    for g in range(KV_HEADS):
        for copy in stores(g):
            copy.wait()


def backward_pass(*arrays):
    wide, narrow = (T, HEADS * D), (T, KV_HEADS * D)
    query, pair = pltpu.HBM(wide, BF16), pltpu.HBM((2,) + narrow, F32)
    return pl.pallas_call(
        backward_kernel,
        in_specs=[IN_HBM] * 8,
        out_specs=(IN_HBM,) * 8,
        out_shape=(query, pair) + (pltpu.HBM(narrow, BF16),) * 2 + (pltpu.HBM((T, WIDE), BF16),) * GROUP,
        scratch_shapes=[pltpu.VMEM(wide, BF16), pltpu.VMEM(narrow, BF16), pltpu.VMEM(narrow, BF16)] * 2
        + [
            pltpu.VMEM((2, KV_HEADS, GROUP * T, D), BF16),
            pltpu.VMEM((2, KV_HEADS, D, D), BF16),
        ]
        + [pltpu.VMEM(wide, BF16), pltpu.VMEM((2,) + narrow, F32), pltpu.VMEM(wide, BF16), pltpu.VMEM((2,) + narrow, BF16)]
        + [pltpu.SemaphoreType.DMA((2, 8)), pltpu.SemaphoreType.DMA((5, KV_HEADS))],
        name="backward_pass",
        cost_estimate=pl.CostEstimate(flops=192 * 2 * D * D * T, bytes_accessed=6 << 20, transcendentals=0),
        compiler_params=PARAMS,
    )(*far(*arrays))


def weight_of(seq, weight_ref):
    return jnp.where(seq == 0, -weight_ref[0:1, 0:1], weight_ref[0:1, 0:1])


def scale_kernel(own_hbm, *refs):
    others, weight_ref, o_hbm = refs[:GROUP], refs[GROUP], refs[GROUP + 1]
    own_ref, scaled_ref, in_sem, out_sems = refs[GROUP + 2 :]
    core = lax.axis_index("core")
    arriving = pltpu.make_async_copy(own_hbm, own_ref, in_sem)
    arriving.start()
    leaving = []
    for turn in (1, 0):
        if turn == 0:
            arriving.wait()
        seq = lax.rem(core + turn, 2)
        weight = weight_of(seq, weight_ref)
        for g in range(GROUP):
            heads = slice(g * WIDE, (g + 1) * WIDE)
            piece = others[g][...] if turn else own_ref[:, heads]
            scaled_ref[turn, :, heads] = (piece.astype(F32) * weight).astype(BF16)
            copy = pltpu.make_async_copy(scaled_ref.at[turn, :, heads], o_hbm.at[0, seq, :, heads], out_sems.at[turn, g])
            copy.start()
            leaving.append(copy)
    for copy in leaving:
        copy.wait()


def scaled_queries(own, others, weight):
    in_vmem = pl.BlockSpec(memory_space=pltpu.VMEM)
    return pl.pallas_call(
        scale_kernel,
        in_specs=[IN_HBM] + [in_vmem] * (GROUP + 1),
        out_specs=IN_HBM,
        out_shape=pltpu.HBM((1, 2, T, HEADS * D), BF16),
        scratch_shapes=[
            pltpu.VMEM((T, HEADS * D), BF16),
            pltpu.VMEM((2, T, HEADS * D), BF16),
            pltpu.SemaphoreType.DMA(()),
            pltpu.SemaphoreType.DMA((2, GROUP)),
        ],
        name="scaled_queries",
        cost_estimate=pl.CostEstimate(flops=2 * T * HEADS * D, bytes_accessed=T, transcendentals=0),
        compiler_params=PARAMS,
    )(*far(own), *near(*others), weight)


def final_kernel(*refs):
    k_ref, v_ref, pair_ref, kg2_ref, vg2_ref, weight_ref = refs[:6]
    after_ref, after2_ref, second_ref, second2_ref = refs[6:10]
    loss_ref, one_ref, two_ref, three_ref, ko_ref, vo_ref, pair_loss_ref = refs[10:]
    pairs = lax.axis_size("dp")
    loss = ((loss_ref[...] + one_ref[...]) + (two_ref[...] + three_ref[...])) / pairs
    pair_loss_ref[0, 0] = jnp.max(loss)
    core = lax.axis_index("core")
    for turn, after, second, key_part, value_part in (
        (0, after_ref, second_ref, pair_ref.at[0], pair_ref.at[1]),
        (1, after2_ref, second2_ref, kg2_ref, vg2_ref),
    ):
        seq = lax.rem(core + turn, 2)
        weight = weight_of(seq, weight_ref)
        for g in range(KV_HEADS):
            span = slice(g * D, (g + 1) * D)
            later = after[g].astype(F32)
            later = jnp.where(core == 0, later + second[g].astype(F32), later).astype(BF16)
            key_grad = key_part[:, span].astype(F32) + dot(v_ref[0, seq, :, span], later, 1, 1)
            value_grad = value_part[:, span].astype(F32) + dot(k_ref[0, seq, :, span], later, 1, 0)
            ko_ref[0, seq, :, span] = (weight * key_grad).astype(BF16)
            vo_ref[0, seq, :, span] = (weight * value_grad).astype(BF16)


def final_pass(*arrays):
    shape = pltpu.HBM((1, 2, T, KV_HEADS * D), BF16)
    return pl.pallas_call(
        final_kernel,
        in_specs=list(out_vmem(14)),
        out_specs=out_vmem(2) + (pl.BlockSpec(memory_space=pltpu.SMEM),),
        out_shape=(shape, shape, jax.ShapeDtypeStruct((1, 1), F32)),
        name="final_pass",
        cost_estimate=pl.CostEstimate(flops=16 * 2 * D * D * T, bytes_accessed=3 << 20, transcendentals=0),
        compiler_params=pltpu.CompilerParams(vmem_limit_bytes=SMALL_VMEM),
    )(*near(*arrays))


def swap(x):
    return lax.ppermute(x, "core", SWAP)


def exchange(x):
    return lax.all_to_all(x, "chip", 0, 0, tiled=True)


def shards(qp, kp, vp, qr, kr, vr, read, mask):
    shared = tuple(swap(x) for x in (kp, vp, kr, vr, mask))
    held = own_states(kp, vp, kr, vr, mask)
    shared, (mine, mask), (qp, qr, read) = lax.optimization_barrier((shared, held, (qp, qr, read)))
    kp2, vp2, kr2, vr2, mask2 = shared
    qp2, qr2, read2 = swap(qp), swap(qr), swap(read)
    total = chip_states(mine, kp2, vp2, kr2, vr2)
    spread = exchange(total)
    before = exchange(exclusive_prefix(spread)).reshape(2, KV_HEADS, D, D)
    own = (qp, qr, read, kp, vp, kr, vr, mask)
    other = (qp2, qr2, read2, kp2, vp2, kr2, vr2, mask2)
    pulled, payload, second, carried = forward_pass(*own, *other, before)
    arrived = exchange(payload)
    qg, pair, kg2, vg2, *qg2 = backward_pass(qp, kp, vp, qp2, kp2, vp2, pulled, carried)
    arrived, qg, pair, qg2, kg2, vg2 = lax.optimization_barrier((arrived, qg, pair, qg2, kg2, vg2))
    after, mine = exclusive_suffix(arrived)
    after, mine, qg2, kg2, vg2, second2 = lax.optimization_barrier(
        (after, mine, qg2, kg2, vg2, second.astype(BF16))
    )
    kg2, vg2, second2 = swap(kg2), swap(vg2), swap(second2)
    qg2 = tuple(swap(x) for x in qg2)
    after = exchange(after).reshape(KV_HEADS, D, D)

    delta = mine + swap(mine)
    loss = jax.nn.softplus(-DPO_BETA * delta)
    pairs = lax.axis_size("dp")
    one, two, three = (lax.ppermute(loss, "dp", [(i, i ^ k) for i in range(pairs)]) for k in (1, 2, 3))
    scale = math.sqrt(HEADS * D * T * lax.axis_size("chip") * 2)
    weight = DPO_BETA * jax.nn.sigmoid(-DPO_BETA * delta) * scale
    query_rows = scaled_queries(qg, qg2, weight)
    after, query_rows, one, two, three = lax.optimization_barrier((after, query_rows, one, two, three))
    key_rows, value_rows, pair_loss = final_pass(
        kp, vp, pair, kg2, vg2, weight, after, swap(after), second, second2, loss, one, two, three
    )
    return query_rows, key_rows, value_rows, pair_loss.reshape(())


def solution(mesh):
    devices = mesh.devices
    split = Mesh(devices.reshape(devices.shape[0] // 2, 2, devices.shape[1]), ("chip", "core", "dp"))
    placed = P("dp", None, ("chip", "core"), None)
    return jax.shard_map(
        shards,
        mesh=split,
        in_specs=(placed,) * 7 + (P("dp", None, ("chip", "core")),),
        out_specs=(placed, placed, placed, P()),
        check_vma=False,
    )
```

```python
import math

import jax
import jax.numpy as jnp
from jax import lax
from jax.experimental import pallas as pl
from jax.experimental.pallas import tpu as pltpu
from jax.sharding import Mesh, PartitionSpec as P

HEADS = 16
KV_HEADS = 4
GROUP = HEADS // KV_HEADS
D = 128
T = 128
DPO_BETA = 0.5
EPS = 1e-06
CHIPS = 32
F32 = jnp.float32
BF16 = jnp.bfloat16
SWAP = [(0, 1), (1, 0)]
SCALAR_ROWS = 8
UNROLL = 4
VMEM_LIMIT = 20 * 1024 * 1024
SMALL_VMEM = 8 * 1024 * 1024


WIDE = GROUP * D
IN_HBM = pl.BlockSpec(memory_space=pltpu.HBM)


def out_vmem(count):
    return (pl.BlockSpec(memory_space=pltpu.VMEM),) * count


def far(*arrays):
    return tuple(pltpu.with_memory_space_constraint(x, pltpu.HBM) for x in arrays)


def near(*arrays):
    return tuple(pltpu.with_memory_space_constraint(x, pltpu.VMEM) for x in arrays)


def dot(a, b, ca, cb):
    return lax.dot_general(a, b, (((ca,), (cb,)), ((), ())), preferred_element_type=F32)


def staged(moves, sems):
    copies = [pltpu.make_async_copy(a, b, sems.at[i]) for i, (a, b) in enumerate(moves)]
    for copy in copies:
        copy.start()
    return copies


def own_states_kernel(*refs):
    own_hbm, mask_hbm, mine_ref, mask_ref, own, sems = refs[:4], refs[4], refs[5], refs[6], refs[7:11], refs[11]
    core = lax.axis_index("core")
    moves = [(a.at[0, core], b) for a, b in zip(own_hbm, own)] + [(mask_hbm, mask_ref)]
    for copy in staged(moves, sems):
        copy.wait()
    for model in range(2):
        for g in range(KV_HEADS):
            span = slice(g * D, (g + 1) * D)
            mine_ref[model, g] = dot(own[2 * model][:, span], own[2 * model + 1][:, span], 0, 0)


def own_states(*arrays):
    return pl.pallas_call(
        own_states_kernel,
        out_shape=(pltpu.VMEM((2, KV_HEADS, D, D), F32), pltpu.VMEM((1, 2, T), jnp.int32)),
        in_specs=[IN_HBM] * 5,
        out_specs=out_vmem(2),
        scratch_shapes=[pltpu.VMEM((T, KV_HEADS * D), BF16)] * 4 + [pltpu.SemaphoreType.DMA((5,))],
        name="own_states",
        cost_estimate=pl.CostEstimate(flops=8 * 2 * D * D * T, bytes_accessed=1 << 20, transcendentals=0),
        compiler_params=pltpu.CompilerParams(vmem_limit_bytes=SMALL_VMEM),
    )(*far(*arrays))


def chip_states_kernel(mine_ref, kp2_ref, vp2_ref, kr2_ref, vr2_ref, total_ref):
    core = lax.axis_index("core")
    rows = 2 * KV_HEADS * D // CHIPS
    for model, (k_ref, v_ref) in enumerate(((kp2_ref, vp2_ref), (kr2_ref, vr2_ref))):
        for g in range(KV_HEADS):
            span = slice(g * D, (g + 1) * D)
            total = mine_ref[model, g] + dot(k_ref[0, core, :, span], v_ref[0, core, :, span], 0, 0)
            total = total.astype(BF16)
            for j in range(D // rows):
                total_ref[(model * KV_HEADS + g) * (D // rows) + j] = total[j * rows : (j + 1) * rows]


def chip_states(*arrays):
    return pl.pallas_call(
        chip_states_kernel,
        out_shape=pltpu.VMEM((CHIPS, 2 * KV_HEADS * D // CHIPS, D), BF16),
        in_specs=[pl.BlockSpec(memory_space=pltpu.VMEM)] * 5,
        out_specs=pl.BlockSpec(memory_space=pltpu.VMEM),
        name="chip_states",
        cost_estimate=pl.CostEstimate(flops=8 * 2 * D * D * T, bytes_accessed=1 << 20, transcendentals=0),
        compiler_params=pltpu.CompilerParams(vmem_limit_bytes=SMALL_VMEM),
    )(*near(*arrays))


def prefix_kernel(x_ref, o_ref):
    total = jnp.zeros(x_ref.shape[1:], F32)
    for chip in range(CHIPS):
        o_ref[chip] = total.astype(BF16)
        total = total + x_ref[chip].astype(F32)


def exclusive_prefix(x):
    return pl.pallas_call(
        prefix_kernel,
        out_shape=pltpu.VMEM(x.shape, BF16),
        in_specs=[pl.BlockSpec(memory_space=pltpu.VMEM)],
        out_specs=pl.BlockSpec(memory_space=pltpu.VMEM),
        name="exclusive_prefix",
        cost_estimate=pl.CostEstimate(flops=x.size, bytes_accessed=4 * x.size, transcendentals=0),
        compiler_params=pltpu.CompilerParams(vmem_limit_bytes=SMALL_VMEM),
    )(*near(x))


def suffix_kernel(x_ref, o_ref, score_ref):
    rows = o_ref.shape[1]
    total = jnp.zeros((rows, D), F32)
    pieces = jnp.zeros((SCALAR_ROWS, D), F32)
    for chip in range(CHIPS - 1, -1, -1):
        o_ref[chip] = total.astype(BF16)
        total = total + x_ref[chip, 0:rows].astype(F32)
        pieces = pieces + x_ref[chip, rows : rows + SCALAR_ROWS].astype(F32)
    score = jnp.broadcast_to(jnp.sum(pieces, axis=0, keepdims=True), (SCALAR_ROWS, D))
    score_ref[...] = jnp.where(lax.axis_index("core") == 0, score, -score)


def exclusive_suffix(x):
    rows = x.shape[1] - SCALAR_ROWS
    return pl.pallas_call(
        suffix_kernel,
        out_shape=(
            pltpu.HBM((CHIPS, rows, D), BF16),
            pltpu.VMEM((SCALAR_ROWS, D), F32),
        ),
        in_specs=[pl.BlockSpec(memory_space=pltpu.VMEM)],
        out_specs=(pl.BlockSpec(memory_space=pltpu.VMEM),) * 2,
        name="exclusive_suffix",
        cost_estimate=pl.CostEstimate(flops=x.size, bytes_accessed=4 * x.size, transcendentals=0),
        compiler_params=pltpu.CompilerParams(vmem_limit_bytes=SMALL_VMEM),
    )(*near(x))


def rows_of(x):
    return jnp.concatenate([x[:, r * D : (r + 1) * D] for r in range(GROUP)], axis=0)


def causal_rows():
    row = lax.broadcasted_iota(jnp.int32, (T, T), 0)
    column = lax.broadcasted_iota(jnp.int32, (T, T), 1)
    return jnp.concatenate([row >= column] * GROUP, axis=0)


def at(g, width):
    return pl.ds(pl.multiple_of(g * width, width), width)


def each_group(body):
    lax.fori_loop(0, KV_HEADS, lambda g, _: (body(g), 0)[1], 0, unroll=UNROLL)


def in_vmem(count):
    return [pl.BlockSpec(memory_space=pltpu.VMEM)] * count


PARAMS = pltpu.CompilerParams(vmem_limit_bytes=VMEM_LIMIT)


def forward_kernel(*refs):
    blocks = (refs[:8], refs[8:16])
    before_ref = refs[16]
    pulled_out, payload_out, second_out, carried_out = refs[17:21]
    pulled_ref, second_ref, carried_ref, acc_ref, total_ref, out_sems, score_sem = refs[21:]
    core = lax.axis_index("core")
    causal = causal_rows()
    row = lax.broadcasted_iota(jnp.int32, (T, T), 0)
    column = lax.broadcasted_iota(jnp.int32, (T, T), 1)
    kept = []
    for block in blocks:
        mask = block[7][0, pl.ds(core, 1), :].astype(F32)
        mask = jnp.sum(jnp.where(row == column, mask, 0.0), axis=1, keepdims=True)
        kept.append(jnp.broadcast_to(mask, (T, D)))

    def masked(read, mask):
        return jnp.concatenate([read[:, r * D : (r + 1) * D].astype(F32) * mask for r in range(GROUP)], axis=0)

    def row_mean(x):
        return jnp.sum(x, axis=1, keepdims=True) * (1.0 / D)

    def carried_of(model, g, states):
        before = before_ref[model, g].astype(F32)
        after = before + jnp.where(core == 0, states[0], states[1])
        own = jnp.where(core == 0, before, after).astype(BF16)
        other = jnp.where(core == 0, after, before).astype(BF16)
        return own, other

    def forward(scores, query, value, carried):
        raw = dot(jnp.concatenate([scores, query], axis=1), jnp.concatenate([value, carried], axis=0), 1, 0)
        inverse = lax.rsqrt(row_mean(raw * raw) + EPS)
        return raw * inverse, inverse

    acc_ref[...] = jnp.zeros_like(acc_ref)
    chunks = CHIPS // KV_HEADS
    rows = D // chunks

    def copies(g):
        return (
            pltpu.make_async_copy(
                total_ref.at[pl.ds(g * chunks, chunks), 0:rows],
                payload_out.at[pl.ds(g * chunks, chunks), 0:rows],
                out_sems.at[3, g],
            ),
            pltpu.make_async_copy(pulled_ref.at[:, g], pulled_out.at[:, g], out_sems.at[0, g]),
            pltpu.make_async_copy(second_ref.at[g], second_out.at[g], out_sems.at[1, g]),
            pltpu.make_async_copy(carried_ref.at[:, g], carried_out.at[:, g], out_sems.at[2, g]),
        )

    def group(g):
        queries, keys, values, scores, carried = [], [], [], [], []
        for model in range(2):
            queries.append([rows_of(b[model][0, core, :, at(g, WIDE)]) for b in blocks])
            keys.append([b[3 + 2 * model][0, core, :, at(g, D)] for b in blocks])
            values.append([b[4 + 2 * model][0, core, :, at(g, D)] for b in blocks])
            states = [dot(k, v, 0, 0) for k, v in zip(keys[model], values[model])]
            carried.append(carried_of(model, g, states))
            scores.append(
                [jnp.where(causal, dot(q, k, 1, 1), 0.0).astype(BF16) for q, k in zip(queries[model], keys[model])]
            )
        tokens = jnp.zeros((1, D), F32)
        grads = []
        for i in range(2):
            query = queries[0][i]
            read = masked(blocks[i][2][0, core, :, at(g, WIDE)], kept[i])
            normed, inverse = forward(scores[0][i], query, values[0][i], carried[0][i])
            normed_ref = forward(scores[1][i], queries[1][i], values[1][i], carried[1][i])[0]
            reading = read * normed
            tokens = tokens + jnp.sum(reading - read * normed_ref, axis=0, keepdims=True)
            pulled = (inverse * (read - normed * row_mean(reading))).astype(BF16)
            pulled_ref[i, g] = pulled
            carried_ref[i, g] = carried[0][i]
            grads.append(dot(query, pulled, 0, 0))
        acc_ref[0:1, :] = acc_ref[0:1, :] + tokens
        total = (grads[0] + grads[1]).astype(BF16)
        for j in range(chunks):
            total_ref[g * chunks + j, 0:rows, :] = total[j * rows : (j + 1) * rows]
        second_ref[g] = jnp.where(core == 0, grads[1], grads[0])
        for copy in copies(g):
            copy.start()

    each_group(group)
    part = jnp.broadcast_to(jnp.sum(acc_ref[0:1, :], axis=1, keepdims=True), (SCALAR_ROWS, D))
    high = part.astype(BF16).astype(F32)
    middle = (part - high).astype(BF16).astype(F32)
    low = part - high - middle
    place = lax.broadcasted_iota(jnp.int32, (SCALAR_ROWS, D), 0)
    pieces = jnp.where(place == 0, high, jnp.where(place == 1, middle, jnp.where(place == 2, low, 0.0))).astype(BF16)
    for chip in range(CHIPS):
        total_ref[chip, rows : rows + SCALAR_ROWS, :] = pieces
    scores_copy = pltpu.make_async_copy(
        total_ref.at[:, rows : rows + SCALAR_ROWS], payload_out.at[:, rows : rows + SCALAR_ROWS], score_sem
    )
    scores_copy.start()
    for g in range(KV_HEADS):
        for copy in copies(g):
            copy.wait()
    scores_copy.wait()


def forward_pass(*arrays):
    rows = KV_HEADS * D // CHIPS + SCALAR_ROWS
    in_vmem = pl.BlockSpec(memory_space=pltpu.VMEM)
    return pl.pallas_call(
        forward_kernel,
        in_specs=[in_vmem] * 17,
        out_specs=(IN_HBM,) * 4,
        out_shape=(
            pltpu.HBM((2, KV_HEADS, GROUP * T, D), BF16),
            pltpu.HBM((CHIPS, rows, D), BF16),
            pltpu.HBM((KV_HEADS, D, D), F32),
            pltpu.HBM((2, KV_HEADS, D, D), BF16),
        ),
        scratch_shapes=[
            pltpu.VMEM((2, KV_HEADS, GROUP * T, D), BF16),
            pltpu.VMEM((KV_HEADS, D, D), F32),
            pltpu.VMEM((2, KV_HEADS, D, D), BF16),
            pltpu.VMEM((8, D), F32),
            pltpu.VMEM((CHIPS, rows, D), BF16),
            pltpu.SemaphoreType.DMA((4, KV_HEADS)),
            pltpu.SemaphoreType.DMA(()),
        ],
        name="forward_pass",
        cost_estimate=pl.CostEstimate(flops=192 * 2 * D * D * T, bytes_accessed=8 << 20, transcendentals=65536),
        compiler_params=PARAMS,
    )(*near(*arrays))


def backward_kernel(*refs):
    (qp_hbm, kp_hbm, vp_hbm, qp2_hbm, kp2_hbm, vp2_hbm, pulled_hbm, carried_hbm) = refs[:8]
    outs = refs[8:16]
    qp_ref, kp_ref, vp_ref, qp2_ref, kp2_ref, vp2_ref, pulled_ref, carried_ref = refs[16:24]
    qg_ref, pair_ref, qg2_ref, pair2_ref, in_sems, out_sems = refs[24:]
    core = lax.axis_index("core")
    causal = causal_rows()

    def load(start, count, sems):
        heads = pl.ds(start * WIDE, count * WIDE)
        shared = pl.ds(start * D, count * D)
        groups = pl.ds(start, count)
        moves = [
            (pulled_hbm.at[:, groups], pulled_ref.at[:, groups]),
            (vp_hbm.at[0, core, :, shared], vp_ref.at[:, shared]),
            (vp2_hbm.at[0, core, :, shared], vp2_ref.at[:, shared]),
            (kp_hbm.at[0, core, :, shared], kp_ref.at[:, shared]),
            (kp2_hbm.at[0, core, :, shared], kp2_ref.at[:, shared]),
            (carried_hbm.at[:, groups], carried_ref.at[:, groups]),
            (qp_hbm.at[0, core, :, heads], qp_ref.at[:, heads]),
            (qp2_hbm.at[0, core, :, heads], qp2_ref.at[:, heads]),
        ]
        return staged(moves, sems)

    def stores(g):
        heads, shared = slice(g * WIDE, (g + 1) * WIDE), slice(g * D, (g + 1) * D)
        held = (
            (qg_ref.at[:, heads], outs[0].at[:, heads]),
            (pair_ref.at[:, :, shared], outs[1].at[:, :, shared]),
            (qg2_ref.at[:, heads], outs[4 + g]),
            (pair2_ref.at[0, :, shared], outs[2].at[:, shared]),
            (pair2_ref.at[1, :, shared], outs[3].at[:, shared]),
        )
        return [pltpu.make_async_copy(a, b, out_sems.at[i, g]) for i, (a, b) in enumerate(held)]

    blocks = ((qp_ref, kp_ref, vp_ref, qg_ref, pair_ref), (qp2_ref, kp2_ref, vp2_ref, qg2_ref, pair2_ref))

    def group(g):
        heads, shared = slice(g * WIDE, (g + 1) * WIDE), slice(g * D, (g + 1) * D)
        for i, (q_ref, k_ref, v_ref, q_out, kv_out) in enumerate(blocks):
            query, key, value = rows_of(q_ref[:, heads]), k_ref[:, shared], v_ref[:, shared]
            pulled = pulled_ref[i, g]
            dscore = jnp.where(causal, dot(pulled, value, 1, 1), 0.0).astype(BF16)
            query_grad = (dot(dscore, key, 1, 0) + dot(pulled, carried_ref[i, g], 1, 1)).astype(BF16)
            q_out[:, heads] = jnp.concatenate([query_grad[r * T : (r + 1) * T] for r in range(GROUP)], axis=1)
            kv_out[0, :, shared] = dot(dscore, query, 0, 0).astype(kv_out.dtype)
            scores = jnp.where(causal, dot(query, key, 1, 1), 0.0).astype(BF16)
            kv_out[1, :, shared] = dot(scores, pulled, 0, 0).astype(kv_out.dtype)
        for copy in stores(g):
            copy.start()

    head = load(0, 1, in_sems.at[0])
    tail = load(1, KV_HEADS - 1, in_sems.at[1])
    for copy in head:
        copy.wait()
    group(0)
    for copy in tail:
        copy.wait()
    for g in range(1, KV_HEADS):
        group(g)
    for g in range(KV_HEADS):
        for copy in stores(g):
            copy.wait()


def backward_pass(*arrays):
    wide, narrow = (T, HEADS * D), (T, KV_HEADS * D)
    query, pair = pltpu.HBM(wide, BF16), pltpu.HBM((2,) + narrow, F32)
    return pl.pallas_call(
        backward_kernel,
        in_specs=[IN_HBM] * 8,
        out_specs=(IN_HBM,) * 8,
        out_shape=(query, pair) + (pltpu.HBM(narrow, BF16),) * 2 + (pltpu.HBM((T, WIDE), BF16),) * GROUP,
        scratch_shapes=[pltpu.VMEM(wide, BF16), pltpu.VMEM(narrow, BF16), pltpu.VMEM(narrow, BF16)] * 2
        + [
            pltpu.VMEM((2, KV_HEADS, GROUP * T, D), BF16),
            pltpu.VMEM((2, KV_HEADS, D, D), BF16),
        ]
        + [pltpu.VMEM(wide, BF16), pltpu.VMEM((2,) + narrow, F32), pltpu.VMEM(wide, BF16), pltpu.VMEM((2,) + narrow, BF16)]
        + [pltpu.SemaphoreType.DMA((2, 8)), pltpu.SemaphoreType.DMA((5, KV_HEADS))],
        name="backward_pass",
        cost_estimate=pl.CostEstimate(flops=192 * 2 * D * D * T, bytes_accessed=6 << 20, transcendentals=0),
        compiler_params=PARAMS,
    )(*far(*arrays))


def weight_of(seq, weight_ref):
    return jnp.where(seq == 0, -weight_ref[0:1, 0:1], weight_ref[0:1, 0:1])


def scale_kernel(own_hbm, *refs):
    others, weight_ref, o_hbm = refs[:GROUP], refs[GROUP], refs[GROUP + 1]
    own_ref, scaled_ref, in_sem, out_sems = refs[GROUP + 2 :]
    core = lax.axis_index("core")
    arriving = pltpu.make_async_copy(own_hbm, own_ref, in_sem)
    arriving.start()
    leaving = []
    for turn in (1, 0):
        if turn == 0:
            arriving.wait()
        seq = lax.rem(core + turn, 2)
        weight = weight_of(seq, weight_ref)
        for g in range(GROUP):
            heads = slice(g * WIDE, (g + 1) * WIDE)
            piece = others[g][...] if turn else own_ref[:, heads]
            scaled_ref[turn, :, heads] = (piece.astype(F32) * weight).astype(BF16)
            copy = pltpu.make_async_copy(scaled_ref.at[turn, :, heads], o_hbm.at[0, seq, :, heads], out_sems.at[turn, g])
            copy.start()
            leaving.append(copy)
    for copy in leaving:
        copy.wait()


def scaled_queries(own, others, weight):
    in_vmem = pl.BlockSpec(memory_space=pltpu.VMEM)
    return pl.pallas_call(
        scale_kernel,
        in_specs=[IN_HBM] + [in_vmem] * (GROUP + 1),
        out_specs=IN_HBM,
        out_shape=pltpu.HBM((1, 2, T, HEADS * D), BF16),
        scratch_shapes=[
            pltpu.VMEM((T, HEADS * D), BF16),
            pltpu.VMEM((2, T, HEADS * D), BF16),
            pltpu.SemaphoreType.DMA(()),
            pltpu.SemaphoreType.DMA((2, GROUP)),
        ],
        name="scaled_queries",
        cost_estimate=pl.CostEstimate(flops=2 * T * HEADS * D, bytes_accessed=T, transcendentals=0),
        compiler_params=PARAMS,
    )(*far(own), *near(*others), weight)


def final_kernel(*refs):
    k_ref, v_ref, pair_ref, kg2_ref, vg2_ref, weight_ref = refs[:6]
    after_ref, after2_ref, second_ref, second2_ref = refs[6:10]
    loss_ref, one_ref, two_ref, three_ref, ko_hbm, vo_hbm, pair_loss_ref, ko_ref, vo_ref, sems = refs[10:]
    leaving = []
    pairs = lax.axis_size("dp")
    loss = ((loss_ref[...] + one_ref[...]) + (two_ref[...] + three_ref[...])) / pairs
    pair_loss_ref[0, 0] = jnp.max(loss)
    core = lax.axis_index("core")
    for turn, after, second, key_part, value_part in (
        (0, after_ref, second_ref, pair_ref.at[0], pair_ref.at[1]),
        (1, after2_ref, second2_ref, kg2_ref, vg2_ref),
    ):
        seq = lax.rem(core + turn, 2)
        weight = weight_of(seq, weight_ref)
        for g in range(KV_HEADS):
            span = slice(g * D, (g + 1) * D)
            later = after[g].astype(F32)
            later = jnp.where(core == 0, later + second[g].astype(F32), later).astype(BF16)
            key_grad = key_part[:, span].astype(F32) + dot(v_ref[0, seq, :, span], later, 1, 1)
            value_grad = value_part[:, span].astype(F32) + dot(k_ref[0, seq, :, span], later, 1, 0)
            ko_ref[turn, :, span] = (weight * key_grad).astype(BF16)
            vo_ref[turn, :, span] = (weight * value_grad).astype(BF16)
        moves = [(ko_ref.at[turn], ko_hbm.at[0, seq]), (vo_ref.at[turn], vo_hbm.at[0, seq])]
        leaving += staged(moves, sems.at[turn])
    for copy in leaving:
        copy.wait()


def final_pass(*arrays):
    shape = pltpu.HBM((1, 2, T, KV_HEADS * D), BF16)
    return pl.pallas_call(
        final_kernel,
        in_specs=list(out_vmem(14)),
        out_specs=(IN_HBM, IN_HBM, pl.BlockSpec(memory_space=pltpu.SMEM)),
        out_shape=(shape, shape, jax.ShapeDtypeStruct((1, 1), F32)),
        scratch_shapes=[pltpu.VMEM((2, T, KV_HEADS * D), BF16)] * 2 + [pltpu.SemaphoreType.DMA((2, 2))],
        name="final_pass",
        cost_estimate=pl.CostEstimate(flops=16 * 2 * D * D * T, bytes_accessed=3 << 20, transcendentals=0),
        compiler_params=pltpu.CompilerParams(vmem_limit_bytes=SMALL_VMEM),
    )(*near(*arrays))


def swap(x):
    return lax.ppermute(x, "core", SWAP)


def exchange(x):
    return lax.all_to_all(x, "chip", 0, 0, tiled=True)


def shards(qp, kp, vp, qr, kr, vr, read, mask):
    shared = tuple(swap(x) for x in (kp, vp, kr, vr, mask))
    held = own_states(kp, vp, kr, vr, mask)
    shared, (mine, mask), (qp, qr, read) = lax.optimization_barrier((shared, held, (qp, qr, read)))
    kp2, vp2, kr2, vr2, mask2 = shared
    qp2, qr2, read2 = swap(qp), swap(qr), swap(read)
    total = chip_states(mine, kp2, vp2, kr2, vr2)
    spread = exchange(total)
    before = exchange(exclusive_prefix(spread)).reshape(2, KV_HEADS, D, D)
    own = (qp, qr, read, kp, vp, kr, vr, mask)
    other = (qp2, qr2, read2, kp2, vp2, kr2, vr2, mask2)
    pulled, payload, second, carried = forward_pass(*own, *other, before)
    arrived = exchange(payload)
    qg, pair, kg2, vg2, *qg2 = backward_pass(qp, kp, vp, qp2, kp2, vp2, pulled, carried)
    arrived, qg, pair, qg2, kg2, vg2 = lax.optimization_barrier((arrived, qg, pair, qg2, kg2, vg2))
    after, mine = exclusive_suffix(arrived)
    after, mine, qg2, kg2, vg2, second2 = lax.optimization_barrier(
        (after, mine, qg2, kg2, vg2, second.astype(BF16))
    )
    kg2, vg2, second2 = swap(kg2), swap(vg2), swap(second2)
    qg2 = tuple(swap(x) for x in qg2)
    after = exchange(after).reshape(KV_HEADS, D, D)

    delta = mine + swap(mine)
    loss = jax.nn.softplus(-DPO_BETA * delta)
    pairs = lax.axis_size("dp")
    one, two, three = (lax.ppermute(loss, "dp", [(i, i ^ k) for i in range(pairs)]) for k in (1, 2, 3))
    scale = math.sqrt(HEADS * D * T * lax.axis_size("chip") * 2)
    weight = DPO_BETA * jax.nn.sigmoid(-DPO_BETA * delta) * scale
    query_rows = scaled_queries(qg, qg2, weight)
    after, query_rows, one, two, three = lax.optimization_barrier((after, query_rows, one, two, three))
    key_rows, value_rows, pair_loss = final_pass(
        kp, vp, pair, kg2, vg2, weight, after, swap(after), second, second2, loss, one, two, three
    )
    return query_rows, key_rows, value_rows, pair_loss.reshape(())


def solution(mesh):
    devices = mesh.devices
    split = Mesh(devices.reshape(devices.shape[0] // 2, 2, devices.shape[1]), ("chip", "core", "dp"))
    placed = P("dp", None, ("chip", "core"), None)
    return jax.shard_map(
        shards,
        mesh=split,
        in_specs=(placed,) * 7 + (P("dp", None, ("chip", "core")),),
        out_specs=(placed, placed, placed, P()),
        check_vma=False,
    )
```
